32 devices in a mesh: vol: 2 (over x), gz: 16 (over z, y, core).
Axes of the slice: x: 2, y: 2, z: 4, core: 2. Of those that a mesh axis runs over, the one named last changes fastest.
Arguments:
- tomogram: float32 [64, 32, 128], P(('vol', 'gz')), parts along dimension 0, may hold values from -120 to 120
- initial_maps: bfloat16 [32, 64, 32, 128], P(None, ('vol', 'gz')), parts along dimension 1, may hold values from -7.2 to 7.2
- dictionary: float32 [32, 64], replicated, may hold values from -0.75 to 0.75
- thresholds: float32 [32], replicated, may hold values from 0.05 to 0.5
Outputs:
- sparse_maps: bfloat16 [32, 64, 32, 128], P(None, ('vol', 'gz')), parts along dimension 1
- descent: float32 [64, 64], P('vol'), parts along dimension 0
- curvature: float32 [2], P('vol'), parts along dimension 0
- residual: float32 [64, 32, 128], P(('vol', 'gz')), parts along dimension 0
The draws below stay inside these ranges and needn't reach their ends.
There are 2 independent parts, one for each index of `vol`. The reference program is written for one: setup_inputs(seed, part) draws one part's arguments, and reference() takes and returns one part's arrays. A program takes and returns all parts, laid end to end along the dimension named above; an argument that names none is the same for every part. Nothing has to cross between parts.
All inputs are finite; a program needn't handle non-finite values.
Results may differ from the reference program's by a relative error of at most 0.012.
Values may be sent and summed in bfloat16 or wider, within the bound.
No kernel may reach another device: no remote copies, remote signals or barrier semaphores. Data moves between devices by JAX's collectives and lax.ppermute only.
A program may use at most 64 MiB of HBM per device.

```python
import math
import jax
import jax.numpy as jnp

ATOMS = 32
TAPS = 64
HEIGHT = 32
BREADTH = 128
DEPTH = 32


def draw_tomogram(key, part):
    noise_key = jax.random.fold_in(key, 11)
    scale_key = jax.random.fold_in(key, 12)
    depth_pos = jnp.arange(DEPTH, dtype=jnp.float32) / DEPTH
    depth_ramp = (2.0 * jnp.exp(math.log(3.0) * depth_pos))[:, None, None]
    row_scale = jnp.exp(jax.random.uniform(scale_key, (DEPTH, HEIGHT, 1), jnp.float32, 0.0, math.log(4.0)))
    noise_part = jnp.clip(jax.random.normal(noise_key, (DEPTH, HEIGHT, BREADTH), jnp.float32), -5.0, 5.0)
    return depth_ramp * row_scale * noise_part


def draw_initial_maps(key, part):
    noise_key = jax.random.fold_in(key, 21)
    depth_pos = jnp.arange(DEPTH, dtype=jnp.float32) / DEPTH
    depth_ramp = (0.6 * jnp.exp(math.log(3.0) * depth_pos))[None, :, None, None]
    noise_part = jnp.clip(jax.random.normal(noise_key, (ATOMS, DEPTH, HEIGHT, BREADTH), jnp.float32), -4.0, 4.0)
    return (depth_ramp * noise_part).astype(jnp.bfloat16)


def bell_draw(stream_key, dims, scale, limit, held_as=jnp.bfloat16):
    return jnp.clip(scale * jax.random.normal(stream_key, dims, jnp.float32), -limit, limit).astype(held_as)


def setup_inputs(seed: int = 0, part: int = 0) -> dict:
    keys = jax.random.split(jax.random.key(seed), 5)
    own_keys = jax.random.split(jax.random.fold_in(keys[4], part), 5)
    tomogram = draw_tomogram(jax.random.fold_in(jax.random.fold_in(keys[4], part), 71), part)
    initial_maps = draw_initial_maps(jax.random.fold_in(jax.random.fold_in(keys[4], part), 71), part)
    dictionary = bell_draw(keys[2], (ATOMS, TAPS), TAPS ** -0.5, 0.75, jnp.float32)
    thresholds = jnp.clip(jnp.exp(jax.random.uniform(keys[3], (ATOMS,), jnp.float32, math.log(0.05), math.log(0.5))), 0.05, 0.5)
    return dict(tomogram=tomogram, initial_maps=initial_maps, dictionary=dictionary, thresholds=thresholds)


coef_step = 0.015
second_t = (1.0 + math.sqrt(5.0)) / 2.0
third_t = (1.0 + math.sqrt(1.0 + 4.0 * second_t * second_t)) / 2.0
momentum = (second_t - 1.0) / third_t

def spread(code_maps, atom_bank):
    atom_count, slab_rows, height, breadth = code_maps.shape
    flattened = code_maps.reshape(atom_count, slab_rows * height * breadth)
    summed = None
    for depth_tap in range(4):
        block_atoms = atom_bank[:, depth_tap * 16:(depth_tap + 1) * 16].T
        partial_terms = jnp.dot(block_atoms, flattened, preferred_element_type=jnp.float32)
        partial_terms = partial_terms.reshape(16, slab_rows, height, breadth)
        for row_tap in range(4):
            for col_tap in range(4):
                widened = jnp.pad(partial_terms[row_tap * 4 + col_tap], ((depth_tap, 3 - depth_tap), (row_tap, 3 - row_tap), (col_tap, 3 - col_tap)))
                shifted = widened[:, 1:height + 1, 1:breadth + 1]
                summed = shifted if summed is None else summed + shifted
    return summed

def unfold(padded, slab_rows, height, breadth, depth_tap):
    pieces = [padded[depth_tap:depth_tap + slab_rows, row_tap:row_tap + height, col_tap:col_tap + breadth] for row_tap in range(4) for col_tap in range(4)]
    return jnp.stack(pieces).reshape(16, slab_rows * height * breadth)

def correlate(padded, atom_bank, slab_rows, height, breadth):
    summed = None
    for depth_tap in range(4):
        term = jnp.dot(atom_bank[:, depth_tap * 16:(depth_tap + 1) * 16], unfold(padded, slab_rows, height, breadth, depth_tap), preferred_element_type=jnp.float32)
        summed = term if summed is None else summed + term
    return summed.reshape(atom_bank.shape[0], slab_rows, height, breadth)

def descent_terms(code_maps, padded):
    atom_count, slab_rows, height, breadth = code_maps.shape
    flattened = code_maps.reshape(atom_count, slab_rows * height * breadth)
    blocks = [jnp.dot(flattened, unfold(padded, slab_rows, height, breadth, depth_tap).T, preferred_element_type=jnp.float32) for depth_tap in range(4)]
    return jnp.concatenate(blocks, axis=1)

def shrink(values, thresholds):
    limits = thresholds[:, None, None, None]
    return values - jnp.clip(values, -limits, limits)

def reference(tomogram, initial_maps, dictionary, thresholds):
    atom_bank = dictionary.astype(jnp.bfloat16)
    depth_rows, height, breadth = tomogram.shape

    def proximal(estimate):
        rebuilt = spread(estimate, atom_bank)[1:depth_rows + 1]
        resid_half = (tomogram - rebuilt).astype(jnp.bfloat16)
        padded = jnp.pad(resid_half, ((1, 2), (1, 2), (1, 2)))
        gradient = correlate(padded, atom_bank, depth_rows, height, breadth)
        return shrink(estimate.astype(jnp.float32) - coef_step * gradient, thresholds).astype(jnp.bfloat16)
    first_maps = proximal(initial_maps)
    first_wide = first_maps.astype(jnp.float32)
    extrapolated = (first_wide + momentum * (first_wide - initial_maps.astype(jnp.float32))).astype(jnp.bfloat16)
    sparse_maps = proximal(extrapolated)
    residual = tomogram - spread(sparse_maps, atom_bank)[1:depth_rows + 1]
    padded = jnp.pad(residual.astype(jnp.bfloat16), ((1, 2), (1, 2), (1, 2)))
    descent = descent_terms(sparse_maps, padded)
    probe = spread(sparse_maps, descent.astype(jnp.bfloat16))[1:depth_rows + 1]
    curvature = jnp.sum(probe * probe).reshape(1)
    return (sparse_maps, descent, curvature, residual)
```

```python
import functools
import math

import jax
import jax.numpy as jnp
from jax import lax
from jax.experimental import pallas as pl
from jax.experimental.pallas import tpu as pltpu
from jax.sharding import PartitionSpec as P

coef_step = 0.015
second_t = (1.0 + math.sqrt(5.0)) / 2.0
third_t = (1.0 + math.sqrt(1.0 + 4.0 * second_t * second_t)) / 2.0
momentum = (second_t - 1.0) / third_t

F32 = jnp.float32
BF16 = jnp.bfloat16
CHUNK = 512


def iota(shape, dim):
    return lax.broadcasted_iota(jnp.int32, shape, dim)


def tap_select(slab, plane, shape, tap_dim):
    tap, col = iota(shape, tap_dim), iota(shape, 1 - tap_dim)
    lands = (2 * slab + plane - 1 + (tap >> 4)) & 7
    return (((tap & 15) == (col >> 3)) & (lands == (col & 7))).astype(BF16)


def taps_dot(lhs, rhs, dims):
    return lax.dot_general(lhs, rhs, (dims, ((), ())), preferred_element_type=F32)


def bank_rows(atoms, slab):
    parts = [taps_dot(atoms, tap_select(slab, z, (64, 128), 0), ((1,), (0,))) for z in range(2)]
    return jnp.concatenate(parts, axis=0).astype(BF16)


def bank_cols(atoms, slab):
    parts = [taps_dot(tap_select(slab, z, (128, 64), 1), atoms, ((1,), (1,))) for z in range(2)]
    return jnp.concatenate(parts, axis=1).astype(BF16)


def spread(bank, maps, products, height, breadth, emit):
    zeros = jnp.zeros((128, 2 * breadth), F32)
    size = height * breadth
    products[:, : 2 * breadth] = zeros
    products[:, 2 * breadth + size :] = zeros[:, :breadth]
    for start in range(0, size, CHUNK):
        products[:, 2 * breadth + start : 2 * breadth + start + CHUNK] = jnp.dot(
            bank, maps[:, start : start + CHUNK], preferred_element_type=F32
        )
    lane = iota((8, breadth), 1)
    for y in range(height):
        sums = []
        for col in range(4):
            terms = [
                products[
                    (4 * row + col) * 8 : (4 * row + col) * 8 + 8,
                    (y + 3 - row) * breadth : (y + 4 - row) * breadth,
                ]
                for row in range(4)
            ]
            sums.append((terms[0] + terms[1]) + (terms[2] + terms[3]))
        total = sums[1] + jnp.where(lane < breadth - 1, pltpu.roll(sums[0], breadth - 1, 1), 0.0)
        total += jnp.where(lane >= 1, pltpu.roll(sums[2], 1, 1), 0.0)
        total += jnp.where(lane >= 2, pltpu.roll(sums[3], 2, 1), 0.0)
        emit(y, total)


def emit_share(slab, tomo, share, height, breadth):
    row = iota((8, breadth), 0)
    first, second = row == ((2 * slab) & 7), row == ((2 * slab + 1) & 7)

    def emit(y, total):
        own = jnp.where(first, tomo[y : y + 1, :], jnp.where(second, tomo[height + y : height + y + 1, :], 0.0))
        share[:, y * breadth : (y + 1) * breadth] = own - total

    return emit


def plane_offset(slab, shape):
    return (iota(shape, 0) - (2 * slab - 1)) & 7


def sent_range(slab, offset):
    low = 2 * (slab & 1)
    return (offset >= low) & (offset <= low + 2)


def gather_resid(slab, slabs, mine, mate, beside, relayed, height, breadth, visit):
    offset = plane_offset(slab, (8, breadth))
    from_beside = sent_range(slab, offset)
    from_relay = offset == 4 * (1 - (slab & 1))
    plane = 2 * slab - 1 + offset
    valid = (offset < 5) & (plane >= 0) & (plane < 2 * slabs)
    for y in range(height):
        cols = slice(y * breadth, (y + 1) * breadth)
        near, far = beside[:, cols], relayed[:, cols]
        total = mine[:, cols] + mate[:, cols]
        total += jnp.where(from_beside, jnp.concatenate([near, near], axis=0), 0.0)
        total += jnp.where(from_relay, jnp.concatenate([far, far], axis=0), 0.0)
        visit(y, jnp.where(valid, total, 0.0))


def unfold(resid, unfolded, height, breadth, y):
    lane = iota((8, breadth), 1)
    shifted = [
        jnp.where(lane >= 1, pltpu.roll(resid, 1, 1), 0.0),
        resid,
        jnp.where(lane < breadth - 1, pltpu.roll(resid, breadth - 1, 1), 0.0),
        jnp.where(lane < breadth - 2, pltpu.roll(resid, breadth - 2, 1), 0.0),
    ]
    halves = [jnp.concatenate(shifted[k : k + 2], axis=0).astype(BF16) for k in (0, 2)]
    for row in range(4):
        target = y - row + 1
        if 0 <= target < height:
            for k in range(2):
                start = row * 32 + k * 16
                unfolded[start : start + 16, target * breadth : (target + 1) * breadth] = halves[k]


def unfold_edges(unfolded, height, breadth):
    zeros = jnp.zeros((32, breadth), BF16)
    for row in range(4):
        for y in range(height):
            if not 0 <= y + row - 1 < height:
                unfolded[row * 32 : row * 32 + 32, y * breadth : (y + 1) * breadth] = zeros


def start_kernel(height, breadth, slab_ref, maps, tomo, atoms, share, by_voxel, rows_out, cols_out, wide, products):
    slab = slab_ref[0]
    atom_count = by_voxel.shape[0] // 2
    bank = atoms[...].astype(BF16)
    rows_out[...] = bank_rows(bank, slab)
    cols = bank_cols(bank, slab)
    cols_out[...] = cols
    wide[...] = maps[...].astype(F32)
    for y in range(height):
        for z in range(2):
            part = wide[pl.ds(z * height + y, atom_count, stride=2 * height), :]
            by_voxel[z * atom_count : (z + 1) * atom_count, y * breadth : (y + 1) * breadth] = part.astype(BF16)
    spread(cols, by_voxel, products, height, breadth, emit_share(slab, tomo, share, height, breadth))


def relay_kernel(slab_ref, mine, mate, out):
    slab = slab_ref[0]
    total = mine[...] + mate[...]
    total = jnp.where(sent_range(slab, plane_offset(slab, total.shape)), total, 0.0)
    out[...] = total[:4] + total[4:]


def step_kernel(height, breadth, slabs, last, slab_ref, mine, mate, beside, relayed, maps, tomo, rows, cols, limits, *rest):
    if last:
        share, by_voxel, natural, unfolded, products, wide = rest
    else:
        share, by_voxel, unfolded, products = rest
    slab = slab_ref[0]
    size = height * breadth
    atom_count = maps.shape[0] // 2
    unfold_edges(unfolded, height, breadth)
    gather_resid(
        slab, slabs, mine, mate, beside, relayed, height, breadth,
        lambda y, resid: unfold(resid, unfolded, height, breadth, y),
    )
    square = (atom_count, atom_count)
    column = jnp.sum(jnp.where(iota(square, 0) == iota(square, 1), limits[...], 0.0), axis=1, keepdims=True)
    limit = jnp.concatenate([column, column], axis=0)
    bank = rows[...]
    for start in range(0, size, CHUNK):
        part = slice(start, start + CHUNK)
        gradient = jnp.dot(bank, unfolded[:, part], preferred_element_type=F32)
        before = maps[:, part].astype(F32)
        moved = before - coef_step * gradient
        after = moved - jnp.clip(moved, -limit, limit)
        if last:
            by_voxel[:, part] = after.astype(BF16)
            for k in range(CHUNK // breadth):
                y = start // breadth + k
                for z in range(2):
                    wide[pl.ds(z * height + y, atom_count, stride=2 * height), :] = after[
                        z * atom_count : (z + 1) * atom_count, k * breadth : (k + 1) * breadth
                    ]
        else:
            after = after.astype(BF16).astype(F32)
            by_voxel[:, part] = (after + momentum * (after - before)).astype(BF16)
    spread(cols[...], by_voxel, products, height, breadth, emit_share(slab, tomo, share, height, breadth))
    if last:
        natural[...] = wide[...].astype(BF16)


def descent_kernel(height, breadth, slabs, slab_ref, mine, mate, beside, relayed, maps, shares, resid_out, unfolded, planes):
    slab = slab_ref[0]
    atom_count = maps.shape[0] // 2
    unfold_edges(unfolded, height, breadth)

    def visit(y, resid):
        planes[8 * y : 8 * y + 8, :] = resid
        unfold(resid, unfolded, height, breadth, y)

    gather_resid(slab, slabs, mine, mate, beside, relayed, height, breadth, visit)
    for z in range(2):
        resid_out[z * height : (z + 1) * height, :] = planes[pl.ds((2 * slab + z) & 7, height, stride=8), :]
    both = taps_dot(maps[...], unfolded[...], ((1,), (1,)))
    total = jnp.zeros((atom_count, 64), F32)
    for z in range(2):
        left = both[z * atom_count : (z + 1) * atom_count, :]
        pick = tap_select(slab, z, (128, 64), 1)
        for _ in range(3):
            head = left.astype(BF16)
            total += taps_dot(head, pick, ((1,), (0,)))
            left = left - head.astype(F32)
    half = atom_count // 2
    packed = jnp.concatenate([total[:half], total[half:]], axis=1)
    for j in range(slabs):
        shares[j] = packed


def probe_kernel(height, breadth, slab_ref, shares, maps, descent_out, share, send, products):
    slab = slab_ref[0]
    packed = jnp.sum(shares[...], axis=0)
    descent = jnp.concatenate([packed[:, :64], packed[:, 64:]], axis=0)
    descent_out[...] = descent

    def emit(y, total):
        share[:, y * breadth : (y + 1) * breadth] = total

    spread(bank_cols(descent.astype(BF16), slab), maps, products, height, breadth, emit)
    total = share[...]
    total = jnp.where(sent_range(slab, plane_offset(slab, total.shape)), total, 0.0)
    send[...] = total[:4] + total[4:]


def square_kernel(slabs, slab_ref, mine, mate, beside, out):
    slab = slab_ref[0]
    offset = plane_offset(slab, mine.shape)
    near = beside[...]
    total = mine[...] + mate[...] + jnp.where(sent_range(slab, offset), jnp.concatenate([near, near], axis=0), 0.0)
    total = jnp.where((offset == 1) | (offset == 2), total * total, 0.0)
    folded = jnp.sum(total, axis=1, keepdims=True)
    out[...] = jnp.broadcast_to(jnp.sum(folded, axis=0, keepdims=True), out.shape)


def call(kernel, outs, operands, scratch=()):
    in_specs = [pl.BlockSpec(memory_space=pltpu.SMEM)] + [pl.BlockSpec(memory_space=pltpu.VMEM)] * (len(operands) - 1)
    return pl.pallas_call(
        kernel,
        out_shape=[jax.ShapeDtypeStruct(shape, dtype) for shape, dtype in outs],
        in_specs=in_specs,
        out_specs=[pl.BlockSpec(memory_space=pltpu.VMEM)] * len(outs),
        scratch_shapes=[pltpu.VMEM(shape, dtype) for shape, dtype in scratch],
    )(*operands)


def per_device(tomogram, initial_maps, dictionary, thresholds):
    slabs = lax.axis_size("gz")
    planes, height, breadth = tomogram.shape
    atom_count = initial_maps.shape[0]
    size = height * breadth
    slab = lax.axis_index("gz").astype(jnp.int32).reshape(1)
    tomo = tomogram.reshape(planes * height, breadth)
    natural = initial_maps.reshape(atom_count * planes * height, breadth)
    limits = thresholds.reshape(1, atom_count)

    mates = [(i, i ^ 1) for i in range(slabs)]
    besides = [(i, i + 1) for i in range(1, slabs - 1, 2)]
    besides += [(j, i) for i, j in besides]

    def to_mate(x):
        return lax.ppermute(x, "gz", mates)

    def to_beside(x):
        return lax.ppermute(x, "gz", besides)

    share_shape = ((8, size), F32)
    maps_shape = ((2 * atom_count, size), BF16)
    products = ((128, size + 3 * breadth), F32)
    unfolded = ((128, size), BF16)
    wide = ((2 * atom_count * height, breadth), F32)
    relay_shape = ((4, size), F32)

    def meet(mine):
        mate = to_mate(mine)
        (send,) = call(relay_kernel, [relay_shape], (slab, mine, mate))
        beside = to_beside(send)
        relayed = to_mate(beside)
        return mine, mate, beside, relayed

    share, maps, rows, cols = call(
        functools.partial(start_kernel, height, breadth),
        [share_shape, maps_shape, ((2 * atom_count, 128), BF16), ((128, 2 * atom_count), BF16)],
        (slab, natural, tomo, dictionary),
        [wide, products],
    )
    share, maps = call(
        functools.partial(step_kernel, height, breadth, slabs, False),
        [share_shape, maps_shape],
        (slab, *meet(share), maps, tomo, rows, cols, limits),
        [unfolded, products],
    )
    share, maps, natural = call(
        functools.partial(step_kernel, height, breadth, slabs, True),
        [share_shape, maps_shape, ((2 * atom_count * height, breadth), BF16)],
        (slab, *meet(share), maps, tomo, rows, cols, limits),
        [unfolded, products, wide],
    )
    shares, residual = call(
        functools.partial(descent_kernel, height, breadth, slabs),
        [((slabs, atom_count // 2, 128), F32), ((planes * height, breadth), F32)],
        (slab, *meet(share), maps),
        [unfolded, ((8 * height, breadth), F32)],
    )
    shares = lax.all_to_all(shares, "gz", 0, 0)
    descent, share, send = call(
        functools.partial(probe_kernel, height, breadth),
        [((atom_count, 64), F32), share_shape, relay_shape],
        (slab, shares, maps),
        [products],
    )
    (norms,) = call(
        functools.partial(square_kernel, slabs),
        [((slabs, 128), F32)],
        (slab, share, to_mate(share), to_beside(send)),
    )
    norms = lax.all_to_all(norms.reshape(slabs, 1, 128), "gz", 0, 0)
    curvature = jnp.sum(norms[:, :, :1]).reshape(1)
    return (
        natural.reshape(initial_maps.shape),
        descent,
        curvature,
        residual.reshape(tomogram.shape),
    )


def solution(mesh):
    return jax.shard_map(
        per_device,
        mesh=mesh,
        in_specs=(P(("vol", "gz"), None, None), P(None, ("vol", "gz"), None, None), P(), P()),
        out_specs=(
            P(None, ("vol", "gz"), None, None),
            P("vol", None),
            P("vol"),
            P(("vol", "gz"), None, None),
        ),
        check_vma=False,
    )
```

```python
import functools
import math

import jax
import jax.numpy as jnp
from jax import lax
from jax.experimental import pallas as pl
from jax.experimental.pallas import tpu as pltpu
from jax.sharding import PartitionSpec as P

coef_step = 0.015
second_t = (1.0 + math.sqrt(5.0)) / 2.0
third_t = (1.0 + math.sqrt(1.0 + 4.0 * second_t * second_t)) / 2.0
momentum = (second_t - 1.0) / third_t

F32 = jnp.float32
BF16 = jnp.bfloat16
CHUNK = 512
VMEM_LIMIT = 16 << 20


def iota(shape, dim):
    return lax.broadcasted_iota(jnp.int32, shape, dim)


def tap_select(slab, plane, shape, tap_dim):
    tap, col = iota(shape, tap_dim), iota(shape, 1 - tap_dim)
    lands = (2 * slab + plane - 1 + (tap >> 4)) & 7
    return (((tap & 15) == (col >> 3)) & (lands == (col & 7))).astype(BF16)


def taps_dot(lhs, rhs, dims):
    return lax.dot_general(lhs, rhs, (dims, ((), ())), preferred_element_type=F32)


def bank_rows(atoms, slab):
    parts = [taps_dot(atoms, tap_select(slab, z, (64, 128), 0), ((1,), (0,))) for z in range(2)]
    return jnp.concatenate(parts, axis=0).astype(BF16)


def bank_cols(atoms, slab):
    parts = [taps_dot(tap_select(slab, z, (128, 64), 1), atoms, ((1,), (1,))) for z in range(2)]
    return jnp.concatenate(parts, axis=1).astype(BF16)


def spread(bank, maps, products, height, breadth, emit):
    zeros = jnp.zeros((128, 2 * breadth), F32)
    size = height * breadth
    products[:, : 2 * breadth] = zeros
    products[:, 2 * breadth + size :] = zeros[:, :breadth]
    for start in range(0, size, CHUNK):
        products[:, 2 * breadth + start : 2 * breadth + start + CHUNK] = jnp.dot(
            bank, maps[:, start : start + CHUNK], preferred_element_type=F32
        )
    lane = iota((8, breadth), 1)
    for y in range(height):
        sums = []
        for col in range(4):
            terms = [
                products[
                    (4 * row + col) * 8 : (4 * row + col) * 8 + 8,
                    (y + 3 - row) * breadth : (y + 4 - row) * breadth,
                ]
                for row in range(4)
            ]
            sums.append((terms[0] + terms[1]) + (terms[2] + terms[3]))
        total = sums[1] + jnp.where(lane < breadth - 1, pltpu.roll(sums[0], breadth - 1, 1), 0.0)
        total += jnp.where(lane >= 1, pltpu.roll(sums[2], 1, 1), 0.0)
        total += jnp.where(lane >= 2, pltpu.roll(sums[3], 2, 1), 0.0)
        emit(y, total)


def emit_share(slab, tomo, share, height, breadth):
    row = iota((8, breadth), 0)
    first, second = row == ((2 * slab) & 7), row == ((2 * slab + 1) & 7)

    def emit(y, total):
        own = jnp.where(first, tomo[y : y + 1, :], jnp.where(second, tomo[height + y : height + y + 1, :], 0.0))
        share[:, y * breadth : (y + 1) * breadth] = own - total

    return emit


def plane_offset(slab, shape):
    return (iota(shape, 0) - (2 * slab - 1)) & 7


def sent_range(slab, offset):
    low = 2 * (slab & 1)
    return (offset >= low) & (offset <= low + 2)


def gather_resid(slab, slabs, mine, mate, beside, relayed, height, breadth, visit):
    offset = plane_offset(slab, (8, breadth))
    from_beside = sent_range(slab, offset)
    from_relay = offset == 4 * (1 - (slab & 1))
    plane = 2 * slab - 1 + offset
    valid = (offset < 5) & (plane >= 0) & (plane < 2 * slabs)
    for y in range(height):
        cols = slice(y * breadth, (y + 1) * breadth)
        near, far = beside[:, cols], relayed[:, cols]
        total = mine[:, cols] + mate[:, cols]
        total += jnp.where(from_beside, jnp.concatenate([near, near], axis=0), 0.0)
        total += jnp.where(from_relay, jnp.concatenate([far, far], axis=0), 0.0)
        visit(y, jnp.where(valid, total, 0.0))


def unfold(resid, unfolded, height, breadth, y):
    lane = iota((8, breadth), 1)
    shifted = [
        jnp.where(lane >= 1, pltpu.roll(resid, 1, 1), 0.0),
        resid,
        jnp.where(lane < breadth - 1, pltpu.roll(resid, breadth - 1, 1), 0.0),
        jnp.where(lane < breadth - 2, pltpu.roll(resid, breadth - 2, 1), 0.0),
    ]
    halves = [jnp.concatenate(shifted[k : k + 2], axis=0).astype(BF16) for k in (0, 2)]
    for row in range(4):
        target = y - row + 1
        if 0 <= target < height:
            for k in range(2):
                start = row * 32 + k * 16
                unfolded[start : start + 16, target * breadth : (target + 1) * breadth] = halves[k]


def unfold_edges(unfolded, height, breadth):
    zeros = jnp.zeros((32, breadth), BF16)
    for row in range(4):
        for y in range(height):
            if not 0 <= y + row - 1 < height:
                unfolded[row * 32 : row * 32 + 32, y * breadth : (y + 1) * breadth] = zeros


def start_kernel(height, breadth, slab_ref, maps, tomo, atoms, share, by_voxel, rows_out, cols_out, wide, products):
    slab = slab_ref[0]
    atom_count = by_voxel.shape[0] // 2
    bank = atoms[...].astype(BF16)
    rows_out[...] = bank_rows(bank, slab)
    cols = bank_cols(bank, slab)
    cols_out[...] = cols
    wide[...] = maps[...].astype(F32)
    for y in range(height):
        for z in range(2):
            part = wide[pl.ds(z * height + y, atom_count, stride=2 * height), :]
            by_voxel[z * atom_count : (z + 1) * atom_count, y * breadth : (y + 1) * breadth] = part.astype(BF16)
    spread(cols, by_voxel, products, height, breadth, emit_share(slab, tomo, share, height, breadth))


def relay_kernel(slab_ref, mine, mate, out):
    slab = slab_ref[0]
    total = mine[...] + mate[...]
    total = jnp.where(sent_range(slab, plane_offset(slab, total.shape)), total, 0.0)
    out[...] = total[:4] + total[4:]


def step_kernel(height, breadth, slabs, last, slab_ref, mine, mate, beside, relayed, maps, tomo, rows, cols, limits, *rest):
    if last:
        share, by_voxel, natural, unfolded, products, wide = rest
    else:
        share, by_voxel, unfolded, products = rest
    slab = slab_ref[0]
    size = height * breadth
    atom_count = maps.shape[0] // 2
    unfold_edges(unfolded, height, breadth)
    gather_resid(
        slab, slabs, mine, mate, beside, relayed, height, breadth,
        lambda y, resid: unfold(resid, unfolded, height, breadth, y),
    )
    square = (atom_count, atom_count)
    column = jnp.sum(jnp.where(iota(square, 0) == iota(square, 1), limits[...], 0.0), axis=1, keepdims=True)
    limit = jnp.concatenate([column, column], axis=0)
    bank = rows[...]
    for start in range(0, size, CHUNK):
        part = slice(start, start + CHUNK)
        gradient = jnp.dot(bank, unfolded[:, part], preferred_element_type=F32)
        before = maps[:, part].astype(F32)
        moved = before - coef_step * gradient
        after = moved - jnp.clip(moved, -limit, limit)
        if last:
            by_voxel[:, part] = after.astype(BF16)
            for k in range(CHUNK // breadth):
                y = start // breadth + k
                for z in range(2):
                    wide[pl.ds(z * height + y, atom_count, stride=2 * height), :] = after[
                        z * atom_count : (z + 1) * atom_count, k * breadth : (k + 1) * breadth
                    ]
        else:
            after = after.astype(BF16).astype(F32)
            by_voxel[:, part] = (after + momentum * (after - before)).astype(BF16)
    spread(cols[...], by_voxel, products, height, breadth, emit_share(slab, tomo, share, height, breadth))
    if last:
        natural[...] = wide[...].astype(BF16)


def descent_kernel(height, breadth, slabs, slab_ref, mine, mate, beside, relayed, maps, shares, resid_out, unfolded, planes):
    slab = slab_ref[0]
    atom_count = maps.shape[0] // 2
    unfold_edges(unfolded, height, breadth)

    def visit(y, resid):
        planes[8 * y : 8 * y + 8, :] = resid
        unfold(resid, unfolded, height, breadth, y)

    gather_resid(slab, slabs, mine, mate, beside, relayed, height, breadth, visit)
    for z in range(2):
        resid_out[z * height : (z + 1) * height, :] = planes[pl.ds((2 * slab + z) & 7, height, stride=8), :]
    both = taps_dot(maps[...], unfolded[...], ((1,), (1,)))
    total = jnp.zeros((atom_count, 64), F32)
    for z in range(2):
        left = both[z * atom_count : (z + 1) * atom_count, :]
        pick = tap_select(slab, z, (128, 64), 1)
        for _ in range(3):
            head = left.astype(BF16)
            total += taps_dot(head, pick, ((1,), (0,)))
            left = left - head.astype(F32)
    half = atom_count // 2
    packed = jnp.concatenate([total[:half], total[half:]], axis=1)
    for j in range(slabs):
        shares[j] = packed


def probe_kernel(height, breadth, slab_ref, shares, maps, descent_out, share, send, products):
    slab = slab_ref[0]
    packed = jnp.sum(shares[...], axis=0)
    descent = jnp.concatenate([packed[:, :64], packed[:, 64:]], axis=0)
    descent_out[...] = descent

    def emit(y, total):
        share[:, y * breadth : (y + 1) * breadth] = total

    spread(bank_cols(descent.astype(BF16), slab), maps, products, height, breadth, emit)
    total = share[...]
    total = jnp.where(sent_range(slab, plane_offset(slab, total.shape)), total, 0.0)
    send[...] = total[:4] + total[4:]


def square_kernel(slabs, slab_ref, mine, mate, beside, out):
    slab = slab_ref[0]
    offset = plane_offset(slab, mine.shape)
    near = beside[...]
    total = mine[...] + mate[...] + jnp.where(sent_range(slab, offset), jnp.concatenate([near, near], axis=0), 0.0)
    total = jnp.where((offset == 1) | (offset == 2), total * total, 0.0)
    folded = jnp.sum(total, axis=1, keepdims=True)
    out[...] = jnp.broadcast_to(jnp.sum(folded, axis=0, keepdims=True), out.shape)


def call(kernel, outs, operands, scratch=()):
    in_specs = [pl.BlockSpec(memory_space=pltpu.SMEM)] + [pl.BlockSpec(memory_space=pltpu.VMEM)] * (len(operands) - 1)
    return pl.pallas_call(
        kernel,
        out_shape=[jax.ShapeDtypeStruct(shape, dtype) for shape, dtype in outs],
        in_specs=in_specs,
        out_specs=[pl.BlockSpec(memory_space=pltpu.VMEM)] * len(outs),
        scratch_shapes=[pltpu.VMEM(shape, dtype) for shape, dtype in scratch],
        compiler_params=pltpu.CompilerParams(vmem_limit_bytes=VMEM_LIMIT),
    )(*operands)


def per_device(tomogram, initial_maps, dictionary, thresholds):
    slabs = lax.axis_size("gz")
    planes, height, breadth = tomogram.shape
    atom_count = initial_maps.shape[0]
    size = height * breadth
    slab = lax.axis_index("gz").astype(jnp.int32).reshape(1)
    tomo = tomogram.reshape(planes * height, breadth)
    natural = initial_maps.reshape(atom_count * planes * height, breadth)
    limits = thresholds.reshape(1, atom_count)

    mates = [(i, i ^ 1) for i in range(slabs)]
    besides = [(i, i + 1) for i in range(1, slabs - 1, 2)]
    besides += [(j, i) for i, j in besides]

    def to_mate(x):
        return lax.ppermute(x, "gz", mates)

    def to_beside(x):
        return lax.ppermute(x, "gz", besides)

    share_shape = ((8, size), F32)
    maps_shape = ((2 * atom_count, size), BF16)
    products = ((128, size + 3 * breadth), F32)
    unfolded = ((128, size), BF16)
    wide = ((2 * atom_count * height, breadth), F32)
    relay_shape = ((4, size), F32)

    def meet(mine):
        mate = to_mate(mine)
        (send,) = call(relay_kernel, [relay_shape], (slab, mine, mate))
        beside = to_beside(send)
        relayed = to_mate(beside)
        return mine, mate, beside, relayed

    share, maps, rows, cols = call(
        functools.partial(start_kernel, height, breadth),
        [share_shape, maps_shape, ((2 * atom_count, 128), BF16), ((128, 2 * atom_count), BF16)],
        (slab, natural, tomo, dictionary),
        [wide, products],
    )
    share, maps = call(
        functools.partial(step_kernel, height, breadth, slabs, False),
        [share_shape, maps_shape],
        (slab, *meet(share), maps, tomo, rows, cols, limits),
        [unfolded, products],
    )
    share, maps, natural = call(
        functools.partial(step_kernel, height, breadth, slabs, True),
        [share_shape, maps_shape, ((2 * atom_count * height, breadth), BF16)],
        (slab, *meet(share), maps, tomo, rows, cols, limits),
        [unfolded, products, wide],
    )
    shares, residual = call(
        functools.partial(descent_kernel, height, breadth, slabs),
        [((slabs, atom_count // 2, 128), F32), ((planes * height, breadth), F32)],
        (slab, *meet(share), maps),
        [unfolded, ((8 * height, breadth), F32)],
    )
    shares = lax.all_to_all(shares, "gz", 0, 0)
    descent, share, send = call(
        functools.partial(probe_kernel, height, breadth),
        [((atom_count, 64), F32), share_shape, relay_shape],
        (slab, shares, maps),
        [products],
    )
    (norms,) = call(
        functools.partial(square_kernel, slabs),
        [((slabs, 128), F32)],
        (slab, share, to_mate(share), to_beside(send)),
    )
    norms = lax.all_to_all(norms.reshape(slabs, 1, 128), "gz", 0, 0)
    curvature = jnp.sum(norms[:, :, :1]).reshape(1)
    return (
        natural.reshape(initial_maps.shape),
        descent,
        curvature,
        residual.reshape(tomogram.shape),
    )


def solution(mesh):
    return jax.shard_map(
        per_device,
        mesh=mesh,
        in_specs=(P(("vol", "gz"), None, None), P(None, ("vol", "gz"), None, None), P(), P()),
        out_specs=(
            P(None, ("vol", "gz"), None, None),
            P("vol", None),
            P("vol"),
            P(("vol", "gz"), None, None),
        ),
        check_vma=False,
    )
```

```python
import functools
import math

import jax
import jax.numpy as jnp
from jax import lax
from jax.experimental import pallas as pl
from jax.experimental.pallas import tpu as pltpu
from jax.sharding import PartitionSpec as P

coef_step = 0.015
second_t = (1.0 + math.sqrt(5.0)) / 2.0
third_t = (1.0 + math.sqrt(1.0 + 4.0 * second_t * second_t)) / 2.0
momentum = (second_t - 1.0) / third_t

F32 = jnp.float32
BF16 = jnp.bfloat16
CHUNK = 512
VMEM_LIMIT = 16 << 20


def iota(shape, dim):
    return lax.broadcasted_iota(jnp.int32, shape, dim)


def tap_select(slab, plane, shape, tap_dim):
    tap, col = iota(shape, tap_dim), iota(shape, 1 - tap_dim)
    lands = (2 * slab + plane - 1 + (tap >> 4)) & 7
    return (((tap & 15) == (col >> 3)) & (lands == (col & 7))).astype(BF16)


def taps_dot(lhs, rhs, dims):
    return lax.dot_general(lhs, rhs, (dims, ((), ())), preferred_element_type=F32)


def bank_rows(atoms, slab):
    parts = [taps_dot(atoms, tap_select(slab, z, (64, 128), 0), ((1,), (0,))) for z in range(2)]
    return jnp.concatenate(parts, axis=0).astype(BF16)


def bank_cols(atoms, slab):
    parts = [taps_dot(tap_select(slab, z, (128, 64), 1), atoms, ((1,), (1,))) for z in range(2)]
    return jnp.concatenate(parts, axis=1).astype(BF16)


def spread(pairs, products, height, breadth, emit):
    zeros = jnp.zeros((128, 2 * breadth), F32)
    size = height * breadth
    products[:, : 2 * breadth] = zeros
    products[:, 2 * breadth + size :] = zeros[:, :breadth]
    for start in range(0, size, CHUNK):
        part = slice(start, start + CHUNK)
        terms = [jnp.dot(bank, maps[:, part], preferred_element_type=F32) for bank, maps in pairs]
        products[:, 2 * breadth + start : 2 * breadth + start + CHUNK] = sum(terms[1:], terms[0])
    lane = iota((8, breadth), 1)
    for y in range(height):
        sums = []
        for col in range(4):
            terms = [
                products[
                    (4 * row + col) * 8 : (4 * row + col) * 8 + 8,
                    (y + 3 - row) * breadth : (y + 4 - row) * breadth,
                ]
                for row in range(4)
            ]
            sums.append((terms[0] + terms[1]) + (terms[2] + terms[3]))
        total = sums[1] + jnp.where(lane < breadth - 1, pltpu.roll(sums[0], breadth - 1, 1), 0.0)
        total += jnp.where(lane >= 1, pltpu.roll(sums[2], 1, 1), 0.0)
        total += jnp.where(lane >= 2, pltpu.roll(sums[3], 2, 1), 0.0)
        emit(y, total)


def emit_share(slab, tomo, share, height, breadth):
    row = iota((8, breadth), 0)
    first, second = row == ((2 * slab) & 7), row == ((2 * slab + 1) & 7)

    def emit(y, total):
        own = jnp.where(first, tomo[y : y + 1, :], jnp.where(second, tomo[height + y : height + y + 1, :], 0.0))
        share[:, y * breadth : (y + 1) * breadth] = own - total

    return emit


def plane_offset(slab, shape):
    return (iota(shape, 0) - (2 * slab - 1)) & 7


def sent_range(slab, offset):
    low = 2 * (slab & 1)
    return (offset >= low) & (offset <= low + 2)


def gather_resid(slab, slabs, mine, mate, beside, relayed, height, breadth, visit):
    offset = plane_offset(slab, (8, breadth))
    from_beside = sent_range(slab, offset)
    from_relay = offset == 4 * (1 - (slab & 1))
    plane = 2 * slab - 1 + offset
    valid = (offset < 5) & (plane >= 0) & (plane < 2 * slabs)
    if relayed is None:
        valid &= ~from_relay
    for y in range(height):
        cols = slice(y * breadth, (y + 1) * breadth)
        near = beside[:, cols]
        total = mine[:, cols] + mate[:, cols]
        total += jnp.where(from_beside, jnp.concatenate([near, near], axis=0), 0.0)
        if relayed is not None:
            far = relayed[:, cols]
            total += jnp.where(from_relay, jnp.concatenate([far, far], axis=0), 0.0)
        visit(y, jnp.where(valid, total, 0.0))


def unfold(resid, unfolded, height, breadth, y):
    lane = iota((8, breadth), 1)
    shifted = [
        jnp.where(lane >= 1, pltpu.roll(resid, 1, 1), 0.0),
        resid,
        jnp.where(lane < breadth - 1, pltpu.roll(resid, breadth - 1, 1), 0.0),
        jnp.where(lane < breadth - 2, pltpu.roll(resid, breadth - 2, 1), 0.0),
    ]
    halves = [jnp.concatenate(shifted[k : k + 2], axis=0).astype(BF16) for k in (0, 2)]
    for row in range(4):
        target = y - row + 1
        if 0 <= target < height:
            for k in range(2):
                start = row * 32 + k * 16
                unfolded[start : start + 16, target * breadth : (target + 1) * breadth] = halves[k]


def unfold_edges(unfolded, height, breadth):
    zeros = jnp.zeros((32, breadth), BF16)
    for row in range(4):
        for y in range(height):
            if not 0 <= y + row - 1 < height:
                unfolded[row * 32 : row * 32 + 32, y * breadth : (y + 1) * breadth] = zeros


def start_kernel(
    height, breadth, slab_ref, maps, tomo, atoms, limits,
    share, by_voxel, rows_out, cols_out, tomo_out, limits_out,
    natural, bank_in, limits_in, wide, products, sems,
):
    slab = slab_ref[0]
    atom_count = by_voxel.shape[0] // 2
    half = maps.shape[0] // 2
    copies = [
        pltpu.make_async_copy(atoms, bank_in, sems.at[0]),
        pltpu.make_async_copy(maps.at[:half], natural.at[:half], sems.at[1]),
        pltpu.make_async_copy(maps.at[half:], natural.at[half:], sems.at[2]),
        pltpu.make_async_copy(tomo, tomo_out, sems.at[3]),
        pltpu.make_async_copy(limits, limits_in, sems.at[4]),
    ]
    for copy in copies:
        copy.start()
    copies[0].wait()
    bank = bank_in[...].astype(BF16)
    rows_out[...] = bank_rows(bank, slab)
    cols = bank_cols(bank, slab)
    cols_out[...] = cols
    group = atom_count // 2
    for part in range(2):
        copies[1 + part].wait()
        span = slice(part * half, (part + 1) * half)
        wide[span, :] = natural[span, :].astype(F32)
        for y in range(height):
            for z in range(2):
                rows = wide[pl.ds(part * half + z * height + y, group, stride=2 * height), :]
                first = z * atom_count + part * group
                by_voxel[first : first + group, y * breadth : (y + 1) * breadth] = rows.astype(BF16)
    copies[3].wait()
    copies[4].wait()
    square = (atom_count, atom_count)
    column = jnp.sum(jnp.where(iota(square, 0) == iota(square, 1), limits_in[...], 0.0), axis=1, keepdims=True)
    limits_out[...] = jnp.broadcast_to(jnp.concatenate([column, column], axis=0), limits_out.shape)
    spread([(cols, by_voxel)], products, height, breadth, emit_share(slab, tomo_out, share, height, breadth))


def relay_kernel(slab_ref, mine, mate, out):
    slab = slab_ref[0]
    total = mine[...] + mate[...]
    total = jnp.where(sent_range(slab, plane_offset(slab, total.shape)), total, 0.0)
    out[...] = total[:4] + total[4:]


def step_kernel(
    height, breadth, slabs, last, slab_ref, mine, mate, beside, relayed, maps, tomo, rows, cols, limits,
    share, by_voxel, unfolded, products,
):
    slab = slab_ref[0]
    size = height * breadth
    unfold_edges(unfolded, height, breadth)
    gather_resid(
        slab, slabs, mine, mate, beside, relayed, height, breadth,
        lambda y, resid: unfold(resid, unfolded, height, breadth, y),
    )
    limit = jnp.concatenate([limits[...]] * (CHUNK // limits.shape[1]), axis=1)
    bank = rows[...]
    for start in range(0, size, CHUNK):
        part = slice(start, start + CHUNK)
        gradient = jnp.dot(bank, unfolded[:, part], preferred_element_type=F32)
        before = maps[:, part].astype(F32)
        moved = before - coef_step * gradient
        after = (moved - jnp.clip(moved, -limit, limit)).astype(BF16)
        if not last:
            after = after.astype(F32)
            after = (after + momentum * (after - before)).astype(BF16)
        by_voxel[:, part] = after
    spread([(cols[...], by_voxel)], products, height, breadth, emit_share(slab, tomo, share, height, breadth))


def natural_kernel(height, breadth, maps, natural, wide):
    atom_count = maps.shape[0] // 2
    for y in range(height):
        rows = maps[:, y * breadth : (y + 1) * breadth].astype(F32)
        for z in range(2):
            wide[pl.ds(z * height + y, atom_count, stride=2 * height), :] = rows[z * atom_count : (z + 1) * atom_count]
    natural[...] = wide[...].astype(BF16)


def descent_kernel(
    height, breadth, slabs, slab_ref, mine, mate, beside, maps, mate_maps, shares, resid_out, unfolded, planes
):
    slab = slab_ref[0]
    odd = slab & 1
    atom_count = maps.shape[0] // 2
    unfold_edges(unfolded, height, breadth)

    def visit(y, resid):
        planes[8 * y : 8 * y + 8, :] = resid
        unfold(resid, unfolded, height, breadth, y)

    gather_resid(slab, slabs, mine, mate, beside, None, height, breadth, visit)
    for z in range(2):
        resid_out[z * height : (z + 1) * height, :] = planes[pl.ds((2 * slab + z) & 7, height, stride=8), :]
    start = pl.multiple_of(odd * atom_count, atom_count)
    terms = [
        (taps_dot(maps[...], unfolded[...], ((1,), (1,))), 0, False),
        (taps_dot(mate_maps[pl.ds(start, atom_count), :], unfolded[...], ((1,), (1,))), 2 - 3 * odd, True),
    ]
    tap = iota((128, 64), 1) >> 4
    total = jnp.zeros((atom_count, 64), F32)
    for both, plane, edge in terms:
        for z in range(both.shape[0] // atom_count):
            left = both[z * atom_count : (z + 1) * atom_count, :]
            pick = tap_select(slab, plane + z, (128, 64), 1)
            if edge:
                pick = jnp.where(tap == 3 * odd, pick, jnp.zeros_like(pick))
            for _ in range(3):
                head = left.astype(BF16)
                total += taps_dot(head, pick, ((1,), (0,)))
                left = left - head.astype(F32)
    half = atom_count // 2
    packed = jnp.concatenate([total[:half], total[half:]], axis=1)
    for j in range(slabs):
        shares[j] = packed


def probe_kernel(height, breadth, slab_ref, shares, maps, mate_maps, beside_maps, descent_out, norms, products, folded):
    slab = slab_ref[0]
    packed = jnp.sum(shares[...], axis=0)
    descent = jnp.concatenate([packed[:, :64], packed[:, 64:]], axis=0)
    descent_out[...] = descent
    half = descent.astype(BF16)
    row = iota((8, breadth), 0)
    own = (row == ((2 * slab) & 7)) | (row == ((2 * slab + 1) & 7))
    odd = slab & 1
    folded[...] = jnp.zeros_like(folded)

    def emit(y, total):
        folded[...] += jnp.where(own, total * total, 0.0)

    pairs = [
        (bank_cols(half, slab), maps),
        (bank_cols(half, slab + 1 - 2 * odd), mate_maps),
        (bank_cols(half, slab - 1 + 2 * odd), beside_maps),
    ]
    spread(pairs, products, height, breadth, emit)
    total = jnp.sum(jnp.sum(folded[...], axis=1, keepdims=True), axis=0, keepdims=True)
    norms[...] = jnp.broadcast_to(total, norms.shape)


def call(kernel, outs, operands, scratch=(), spaces=None):
    spaces = spaces or [pltpu.SMEM] + [pltpu.VMEM] * (len(operands) - 1)
    return pl.pallas_call(
        kernel,
        out_shape=[jax.ShapeDtypeStruct(shape, dtype) for shape, dtype in outs],
        in_specs=[pl.BlockSpec(memory_space=space) for space in spaces],
        out_specs=[pl.BlockSpec(memory_space=pltpu.VMEM)] * len(outs),
        scratch_shapes=[pltpu.VMEM(*item) if isinstance(item, tuple) else item for item in scratch],
        compiler_params=pltpu.CompilerParams(vmem_limit_bytes=VMEM_LIMIT),
    )(*operands)


def per_device(tomogram, initial_maps, dictionary, thresholds):
    slabs = lax.axis_size("gz")
    planes, height, breadth = tomogram.shape
    atom_count = initial_maps.shape[0]
    size = height * breadth
    slab = lax.axis_index("gz").astype(jnp.int32).reshape(1)
    tomo = tomogram.reshape(planes * height, breadth)
    natural = initial_maps.reshape(atom_count * planes * height, breadth)
    limits = thresholds.reshape(1, atom_count)
    natural, tomo, dictionary, limits = (
        pltpu.with_memory_space_constraint(x, pltpu.HBM) for x in (natural, tomo, dictionary, limits)
    )

    mates = [(i, i ^ 1) for i in range(slabs)]
    besides = [(i, i + 1) for i in range(1, slabs - 1, 2)]
    besides += [(j, i) for i, j in besides]

    def to_mate(x):
        return lax.ppermute(x, "gz", mates)

    def to_beside(x):
        return lax.ppermute(x, "gz", besides)

    share_shape = ((8, size), F32)
    maps_shape = ((2 * atom_count, size), BF16)
    natural_shape = (natural.shape, BF16)
    products = ((128, size + 3 * breadth), F32)
    unfolded = ((128, size), BF16)
    wide = (natural.shape, F32)

    def meet(mine):
        mate = to_mate(mine)
        (send,) = call(relay_kernel, [((4, size), F32)], (slab, mine, mate))
        return mine, mate, send

    def step(share, maps, last):
        mine, mate, send = meet(share)
        beside = to_beside(send)
        return call(
            functools.partial(step_kernel, height, breadth, slabs, last),
            [share_shape, maps_shape],
            (slab, mine, mate, beside, to_mate(beside), maps, tomo, rows, cols, limits),
            [unfolded, products],
        )

    share, maps, rows, cols, tomo, limits = call(
        functools.partial(start_kernel, height, breadth),
        [
            share_shape,
            maps_shape,
            ((2 * atom_count, 128), BF16),
            ((128, 2 * atom_count), BF16),
            (tomo.shape, F32),
            ((2 * atom_count, 128), F32),
        ],
        (slab, natural, tomo, dictionary, limits),
        [
            natural_shape,
            (dictionary.shape, F32),
            (limits.shape, F32),
            wide,
            products,
            pltpu.SemaphoreType.DMA((5,)),
        ],
        [pltpu.SMEM] + [pltpu.HBM] * 4,
    )
    share, maps = step(share, maps, False)
    share, maps = step(share, maps, True)
    mine, mate, send = meet(share)
    send, maps = lax.optimization_barrier((send, maps))
    beside = to_beside(send)
    mate_maps = to_mate(maps)
    beside_maps = to_beside(maps)
    (natural,) = call(
        functools.partial(natural_kernel, height, breadth), [natural_shape], (maps,), [wide], [pltpu.VMEM]
    )
    shares, residual = call(
        functools.partial(descent_kernel, height, breadth, slabs),
        [((slabs, atom_count // 2, 128), F32), (tomo.shape, F32)],
        (slab, mine, mate, beside, maps, mate_maps),
        [unfolded, ((8 * height, breadth), F32)],
    )
    shares = lax.all_to_all(shares, "gz", 0, 0)
    descent, norms = call(
        functools.partial(probe_kernel, height, breadth),
        [((atom_count, 64), F32), ((slabs, 128), F32)],
        (slab, shares, maps, mate_maps, beside_maps),
        [products, ((8, breadth), F32)],
    )
    norms = lax.all_to_all(norms.reshape(slabs, 1, 128), "gz", 0, 0)
    curvature = jnp.sum(norms[:, :, :1]).reshape(1)
    return (
        natural.reshape(initial_maps.shape),
        descent,
        curvature,
        residual.reshape(tomogram.shape),
    )


def solution(mesh):
    return jax.shard_map(
        per_device,
        mesh=mesh,
        in_specs=(P(("vol", "gz"), None, None), P(None, ("vol", "gz"), None, None), P(), P()),
        out_specs=(
            P(None, ("vol", "gz"), None, None),
            P("vol", None),
            P("vol"),
            P(("vol", "gz"), None, None),
        ),
        check_vma=False,
    )
```

```python
import functools
import math

import jax
import jax.numpy as jnp
from jax import lax
from jax.experimental import pallas as pl
from jax.experimental.pallas import tpu as pltpu
from jax.sharding import PartitionSpec as P

coef_step = 0.015
second_t = (1.0 + math.sqrt(5.0)) / 2.0
third_t = (1.0 + math.sqrt(1.0 + 4.0 * second_t * second_t)) / 2.0
momentum = (second_t - 1.0) / third_t

F32 = jnp.float32
BF16 = jnp.bfloat16
CHUNK = 512
VMEM_LIMIT = 16 << 20


def iota(shape, dim):
    return lax.broadcasted_iota(jnp.int32, shape, dim)


def tap_select(slab, plane, shape, tap_dim):
    tap, col = iota(shape, tap_dim), iota(shape, 1 - tap_dim)
    lands = (2 * slab + plane - 1 + (tap >> 4)) & 7
    return (((tap & 15) == (col >> 3)) & (lands == (col & 7))).astype(BF16)


def taps_dot(lhs, rhs, dims):
    return lax.dot_general(lhs, rhs, (dims, ((), ())), preferred_element_type=F32)


def bank_rows(atoms, slab):
    parts = [taps_dot(atoms, tap_select(slab, z, (64, 128), 0), ((1,), (0,))) for z in range(2)]
    return jnp.concatenate(parts, axis=0).astype(BF16)


def bank_cols(atoms, slab):
    parts = [taps_dot(tap_select(slab, z, (128, 64), 1), atoms, ((1,), (1,))) for z in range(2)]
    return jnp.concatenate(parts, axis=1).astype(BF16)


def spread(pairs, products, height, breadth, emit):
    zeros = jnp.zeros((128, 2 * breadth), F32)
    size = height * breadth
    products[:, : 2 * breadth] = zeros
    products[:, 2 * breadth + size :] = zeros[:, :breadth]
    for start in range(0, size, CHUNK):
        part = slice(start, start + CHUNK)
        terms = [jnp.dot(bank, maps[:, part], preferred_element_type=F32) for bank, maps in pairs]
        products[:, 2 * breadth + start : 2 * breadth + start + CHUNK] = sum(terms[1:], terms[0])
    lane = iota((8, breadth), 1)
    for y in range(height):
        sums = []
        for col in range(4):
            terms = [
                products[
                    (4 * row + col) * 8 : (4 * row + col) * 8 + 8,
                    (y + 3 - row) * breadth : (y + 4 - row) * breadth,
                ]
                for row in range(4)
            ]
            sums.append((terms[0] + terms[1]) + (terms[2] + terms[3]))
        total = sums[1] + jnp.where(lane < breadth - 1, pltpu.roll(sums[0], breadth - 1, 1), 0.0)
        total += jnp.where(lane >= 1, pltpu.roll(sums[2], 1, 1), 0.0)
        total += jnp.where(lane >= 2, pltpu.roll(sums[3], 2, 1), 0.0)
        emit(y, total)


def emit_share(slab, tomo, share, height, breadth):
    row = iota((8, breadth), 0)
    first, second = row == ((2 * slab) & 7), row == ((2 * slab + 1) & 7)

    def emit(y, total):
        own = jnp.where(first, tomo[y : y + 1, :], jnp.where(second, tomo[height + y : height + y + 1, :], 0.0))
        share[:, y * breadth : (y + 1) * breadth] = own - total

    return emit


def plane_offset(slab, shape):
    return (iota(shape, 0) - (2 * slab - 1)) & 7


def sent_range(slab, offset):
    low = 2 * (slab & 1)
    return (offset >= low) & (offset <= low + 2)


def gather_resid(slab, slabs, mine, mate, beside, relayed, height, breadth, visit):
    offset = plane_offset(slab, (8, breadth))
    odd = slab & 1
    edge = slab + 1 - 2 * odd
    from_beside = sent_range(slab, offset) & (slab > 0) & (slab < slabs - 1)
    from_relay = (offset == 4 * (1 - odd)) & (edge > 0) & (edge < slabs - 1)
    plane = 2 * slab - 1 + offset
    valid = (offset < 5) & (plane >= 0) & (plane < 2 * slabs)
    if relayed is None:
        valid &= offset != 4 * (1 - odd)
    for y in range(height):
        cols = slice(y * breadth, (y + 1) * breadth)
        near = beside[:, cols]
        total = mine[:, cols] + mate[:, cols]
        total += jnp.where(from_beside, jnp.concatenate([near, near], axis=0), 0.0)
        if relayed is not None:
            far = relayed[:, cols]
            total += jnp.where(from_relay, jnp.concatenate([far, far], axis=0), 0.0)
        visit(y, jnp.where(valid, total, 0.0))


def unfold(resid, unfolded, height, breadth, y):
    lane = iota((8, breadth), 1)
    shifted = [
        jnp.where(lane >= 1, pltpu.roll(resid, 1, 1), 0.0),
        resid,
        jnp.where(lane < breadth - 1, pltpu.roll(resid, breadth - 1, 1), 0.0),
        jnp.where(lane < breadth - 2, pltpu.roll(resid, breadth - 2, 1), 0.0),
    ]
    halves = [jnp.concatenate(shifted[k : k + 2], axis=0).astype(BF16) for k in (0, 2)]
    for row in range(4):
        target = y - row + 1
        if 0 <= target < height:
            for k in range(2):
                start = row * 32 + k * 16
                unfolded[start : start + 16, target * breadth : (target + 1) * breadth] = halves[k]


def unfold_edges(unfolded, height, breadth):
    zeros = jnp.zeros((32, breadth), BF16)
    for row in range(4):
        for y in range(height):
            if not 0 <= y + row - 1 < height:
                unfolded[row * 32 : row * 32 + 32, y * breadth : (y + 1) * breadth] = zeros


def start_kernel(
    height, breadth, slab_ref, maps, tomo, atoms, limits,
    share, by_voxel, rows_out, cols_out, tomo_out, limits_out,
    natural, bank_in, limits_in, wide, products, sems,
):
    slab = slab_ref[0]
    atom_count = by_voxel.shape[0] // 2
    half = maps.shape[0] // 2
    copies = [
        pltpu.make_async_copy(atoms, bank_in, sems.at[0]),
        pltpu.make_async_copy(maps.at[:half], natural.at[:half], sems.at[1]),
        pltpu.make_async_copy(maps.at[half:], natural.at[half:], sems.at[2]),
        pltpu.make_async_copy(tomo, tomo_out, sems.at[3]),
        pltpu.make_async_copy(limits, limits_in, sems.at[4]),
    ]
    for copy in copies:
        copy.start()
    copies[0].wait()
    bank = bank_in[...].astype(BF16)
    rows_out[...] = bank_rows(bank, slab)
    cols = bank_cols(bank, slab)
    cols_out[...] = cols
    group = atom_count // 2
    for part in range(2):
        copies[1 + part].wait()
        span = slice(part * half, (part + 1) * half)
        wide[span, :] = natural[span, :].astype(F32)
        for y in range(height):
            for z in range(2):
                rows = wide[pl.ds(part * half + z * height + y, group, stride=2 * height), :]
                first = z * atom_count + part * group
                by_voxel[first : first + group, y * breadth : (y + 1) * breadth] = rows.astype(BF16)
    copies[3].wait()
    copies[4].wait()
    square = (atom_count, atom_count)
    column = jnp.sum(jnp.where(iota(square, 0) == iota(square, 1), limits_in[...], 0.0), axis=1, keepdims=True)
    limits_out[...] = jnp.broadcast_to(jnp.concatenate([column, column], axis=0), limits_out.shape)
    spread([(cols, by_voxel)], products, height, breadth, emit_share(slab, tomo_out, share, height, breadth))


def relay_kernel(slab_ref, mine, mate, out):
    slab = slab_ref[0]
    total = mine[...] + mate[...]
    total = jnp.where(sent_range(slab, plane_offset(slab, total.shape)), total, 0.0)
    out[...] = total[:4] + total[4:]


def step_kernel(
    height, breadth, slabs, last, slab_ref, mine, mate, beside, relayed, maps, tomo, rows, cols, limits,
    share, by_voxel, unfolded, products,
):
    slab = slab_ref[0]
    size = height * breadth
    unfold_edges(unfolded, height, breadth)
    gather_resid(
        slab, slabs, mine, mate, beside, relayed, height, breadth,
        lambda y, resid: unfold(resid, unfolded, height, breadth, y),
    )
    limit = jnp.concatenate([limits[...]] * (CHUNK // limits.shape[1]), axis=1)
    bank = rows[...]
    for start in range(0, size, CHUNK):
        part = slice(start, start + CHUNK)
        gradient = jnp.dot(bank, unfolded[:, part], preferred_element_type=F32)
        before = maps[:, part].astype(F32)
        moved = before - coef_step * gradient
        after = (moved - jnp.clip(moved, -limit, limit)).astype(BF16)
        if not last:
            after = after.astype(F32)
            after = (after + momentum * (after - before)).astype(BF16)
        by_voxel[:, part] = after
    spread([(cols[...], by_voxel)], products, height, breadth, emit_share(slab, tomo, share, height, breadth))


def natural_kernel(height, breadth, maps, natural, wide):
    atom_count = maps.shape[0] // 2
    for y in range(height):
        rows = maps[:, y * breadth : (y + 1) * breadth].astype(F32)
        for z in range(2):
            wide[pl.ds(z * height + y, atom_count, stride=2 * height), :] = rows[z * atom_count : (z + 1) * atom_count]
    natural[...] = wide[...].astype(BF16)


def descent_kernel(
    height, breadth, slabs, slab_ref, mine, mate, beside, maps, mate_maps, shares, resid_out, unfolded, planes
):
    slab = slab_ref[0]
    odd = slab & 1
    atom_count = maps.shape[0] // 2
    unfold_edges(unfolded, height, breadth)

    def visit(y, resid):
        planes[8 * y : 8 * y + 8, :] = resid
        unfold(resid, unfolded, height, breadth, y)

    gather_resid(slab, slabs, mine, mate, beside, None, height, breadth, visit)
    for z in range(2):
        resid_out[z * height : (z + 1) * height, :] = planes[pl.ds((2 * slab + z) & 7, height, stride=8), :]
    start = pl.multiple_of(odd * atom_count, atom_count)
    terms = [
        (taps_dot(maps[...], unfolded[...], ((1,), (1,))), 0, False),
        (taps_dot(mate_maps[pl.ds(start, atom_count), :], unfolded[...], ((1,), (1,))), 2 - 3 * odd, True),
    ]
    tap = iota((128, 64), 1) >> 4
    total = jnp.zeros((atom_count, 64), F32)
    for both, plane, edge in terms:
        for z in range(both.shape[0] // atom_count):
            left = both[z * atom_count : (z + 1) * atom_count, :]
            pick = tap_select(slab, plane + z, (128, 64), 1)
            if edge:
                pick = jnp.where(tap == 3 * odd, pick, jnp.zeros_like(pick))
            for _ in range(3):
                head = left.astype(BF16)
                total += taps_dot(head, pick, ((1,), (0,)))
                left = left - head.astype(F32)
    half = atom_count // 2
    packed = jnp.concatenate([total[:half], total[half:]], axis=1)
    for j in range(slabs):
        shares[j] = packed


def probe_kernel(height, breadth, slabs, slab_ref, shares, maps, mate_maps, beside_maps, descent_out, norms, products, folded):
    slab = slab_ref[0]
    packed = jnp.sum(shares[...], axis=0)
    descent = jnp.concatenate([packed[:, :64], packed[:, 64:]], axis=0)
    descent_out[...] = descent
    half = descent.astype(BF16)
    row = iota((8, breadth), 0)
    own = (row == ((2 * slab) & 7)) | (row == ((2 * slab + 1) & 7))
    odd = slab & 1
    folded[...] = jnp.zeros_like(folded)

    def emit(y, total):
        folded[...] += jnp.where(own, total * total, 0.0)

    beside_bank = bank_cols(half, slab - 1 + 2 * odd)
    pairs = [
        (bank_cols(half, slab), maps),
        (bank_cols(half, slab + 1 - 2 * odd), mate_maps),
        (jnp.where((slab > 0) & (slab < slabs - 1), beside_bank, jnp.zeros_like(beside_bank)), beside_maps),
    ]
    spread(pairs, products, height, breadth, emit)
    total = jnp.sum(jnp.sum(folded[...], axis=1, keepdims=True), axis=0, keepdims=True)
    norms[...] = jnp.broadcast_to(total, norms.shape)


def call(kernel, outs, operands, scratch=(), spaces=None):
    spaces = spaces or [pltpu.SMEM] + [pltpu.VMEM] * (len(operands) - 1)
    return pl.pallas_call(
        kernel,
        out_shape=[jax.ShapeDtypeStruct(shape, dtype) for shape, dtype in outs],
        in_specs=[pl.BlockSpec(memory_space=space) for space in spaces],
        out_specs=[pl.BlockSpec(memory_space=pltpu.VMEM)] * len(outs),
        scratch_shapes=[pltpu.VMEM(*item) if isinstance(item, tuple) else item for item in scratch],
        compiler_params=pltpu.CompilerParams(vmem_limit_bytes=VMEM_LIMIT),
    )(*operands)


def per_device(tomogram, initial_maps, dictionary, thresholds):
    slabs = lax.axis_size("gz")
    planes, height, breadth = tomogram.shape
    atom_count = initial_maps.shape[0]
    size = height * breadth
    slab = lax.axis_index("gz").astype(jnp.int32).reshape(1)
    tomo = tomogram.reshape(planes * height, breadth)
    natural = initial_maps.reshape(atom_count * planes * height, breadth)
    limits = thresholds.reshape(1, atom_count)
    natural, tomo, dictionary, limits = (
        pltpu.with_memory_space_constraint(x, pltpu.HBM) for x in (natural, tomo, dictionary, limits)
    )

    mates = [(i, i ^ 1) for i in range(slabs)]
    parts = lax.axis_size("vol")
    besides = [(v * slabs + i, v * slabs + i + 1) for v in range(parts) for i in range(1, slabs - 1, 2)]
    besides += [(v * slabs + i, (v + 1) * slabs + i) for v in range(0, parts - 1, 2) for i in (0, slabs - 1)]
    besides += [(j, i) for i, j in besides]

    def to_mate(x):
        return lax.ppermute(x, "gz", mates)

    def to_beside(x):
        return lax.ppermute(x, ("vol", "gz"), besides)

    share_shape = ((8, size), F32)
    maps_shape = ((2 * atom_count, size), BF16)
    natural_shape = (natural.shape, BF16)
    products = ((128, size + 3 * breadth), F32)
    unfolded = ((128, size), BF16)
    wide = (natural.shape, F32)

    def meet(mine):
        mate = to_mate(mine)
        (send,) = call(relay_kernel, [((4, size), F32)], (slab, mine, mate))
        return mine, mate, send

    def step(share, maps, last):
        mine, mate, send = meet(share)
        beside = to_beside(send)
        return call(
            functools.partial(step_kernel, height, breadth, slabs, last),
            [share_shape, maps_shape],
            (slab, mine, mate, beside, to_mate(beside), maps, tomo, rows, cols, limits),
            [unfolded, products],
        )

    share, maps, rows, cols, tomo, limits = call(
        functools.partial(start_kernel, height, breadth),
        [
            share_shape,
            maps_shape,
            ((2 * atom_count, 128), BF16),
            ((128, 2 * atom_count), BF16),
            (tomo.shape, F32),
            ((2 * atom_count, 128), F32),
        ],
        (slab, natural, tomo, dictionary, limits),
        [
            natural_shape,
            (dictionary.shape, F32),
            (limits.shape, F32),
            wide,
            products,
            pltpu.SemaphoreType.DMA((5,)),
        ],
        [pltpu.SMEM] + [pltpu.HBM] * 4,
    )
    share, maps = step(share, maps, False)
    share, maps = step(share, maps, True)
    mine, mate, send = meet(share)
    send, maps = lax.optimization_barrier((send, maps))
    beside = to_beside(send)
    mate_maps = to_mate(maps)
    beside_maps = to_beside(maps)
    (natural,) = call(
        functools.partial(natural_kernel, height, breadth), [natural_shape], (maps,), [wide], [pltpu.VMEM]
    )
    shares, residual = call(
        functools.partial(descent_kernel, height, breadth, slabs),
        [((slabs, atom_count // 2, 128), F32), (tomo.shape, F32)],
        (slab, mine, mate, beside, maps, mate_maps),
        [unfolded, ((8 * height, breadth), F32)],
    )
    shares = lax.all_to_all(shares, "gz", 0, 0)
    descent, norms = call(
        functools.partial(probe_kernel, height, breadth, slabs),
        [((atom_count, 64), F32), ((slabs, 128), F32)],
        (slab, shares, maps, mate_maps, beside_maps),
        [products, ((8, breadth), F32)],
    )
    norms = lax.all_to_all(norms.reshape(slabs, 1, 128), "gz", 0, 0)
    curvature = jnp.sum(norms[:, :, :1]).reshape(1)
    return (
        natural.reshape(initial_maps.shape),
        descent,
        curvature,
        residual.reshape(tomogram.shape),
    )


def solution(mesh):
    return jax.shard_map(
        per_device,
        mesh=mesh,
        in_specs=(P(("vol", "gz"), None, None), P(None, ("vol", "gz"), None, None), P(), P()),
        out_specs=(
            P(None, ("vol", "gz"), None, None),
            P("vol", None),
            P("vol"),
            P(("vol", "gz"), None, None),
        ),
        check_vma=False,
    )
```

```python
import functools
import math

import jax
import jax.numpy as jnp
from jax import lax
from jax.experimental import pallas as pl
from jax.experimental.pallas import tpu as pltpu
from jax.sharding import PartitionSpec as P

coef_step = 0.015
second_t = (1.0 + math.sqrt(5.0)) / 2.0
third_t = (1.0 + math.sqrt(1.0 + 4.0 * second_t * second_t)) / 2.0
momentum = (second_t - 1.0) / third_t

F32 = jnp.float32
BF16 = jnp.bfloat16
CHUNK = 512
VMEM_LIMIT = 16 << 20


def iota(shape, dim):
    return lax.broadcasted_iota(jnp.int32, shape, dim)


def tap_select(slab, plane, shape, tap_dim):
    tap, col = iota(shape, tap_dim), iota(shape, 1 - tap_dim)
    lands = (2 * slab + plane - 1 + (tap >> 4)) & 7
    return (((tap & 15) == (col >> 3)) & (lands == (col & 7))).astype(BF16)


def taps_dot(lhs, rhs, dims):
    return lax.dot_general(lhs, rhs, (dims, ((), ())), preferred_element_type=F32)


def bank_rows(atoms, slab):
    parts = [taps_dot(atoms, tap_select(slab, z, (64, 128), 0), ((1,), (0,))) for z in range(2)]
    return jnp.concatenate(parts, axis=0).astype(BF16)


def bank_cols(atoms, slab):
    parts = [taps_dot(tap_select(slab, z, (128, 64), 1), atoms, ((1,), (1,))) for z in range(2)]
    return jnp.concatenate(parts, axis=1).astype(BF16)


def spread(pairs, products, height, breadth, emit):
    zeros = jnp.zeros((128, 2 * breadth), F32)
    size = height * breadth
    products[:, : 2 * breadth] = zeros
    products[:, 2 * breadth + size :] = zeros[:, :breadth]
    for start in range(0, size, CHUNK):
        part = slice(start, start + CHUNK)
        terms = [jnp.dot(bank, maps[:, part], preferred_element_type=F32) for bank, maps in pairs]
        products[:, 2 * breadth + start : 2 * breadth + start + CHUNK] = sum(terms[1:], terms[0])
    lane = iota((8, breadth), 1)
    for y in range(height):
        sums = []
        for col in range(4):
            terms = [
                products[
                    (4 * row + col) * 8 : (4 * row + col) * 8 + 8,
                    (y + 3 - row) * breadth : (y + 4 - row) * breadth,
                ]
                for row in range(4)
            ]
            sums.append((terms[0] + terms[1]) + (terms[2] + terms[3]))
        total = sums[1] + jnp.where(lane < breadth - 1, pltpu.roll(sums[0], breadth - 1, 1), 0.0)
        total += jnp.where(lane >= 1, pltpu.roll(sums[2], 1, 1), 0.0)
        total += jnp.where(lane >= 2, pltpu.roll(sums[3], 2, 1), 0.0)
        emit(y, total)


def emit_share(slab, tomo, share, height, breadth):
    row = iota((8, breadth), 0)
    first, second = row == ((2 * slab) & 7), row == ((2 * slab + 1) & 7)

    def emit(y, total):
        own = jnp.where(first, tomo[y : y + 1, :], jnp.where(second, tomo[height + y : height + y + 1, :], 0.0))
        share[:, y * breadth : (y + 1) * breadth] = own - total

    return emit


def plane_offset(slab, shape):
    return (iota(shape, 0) - (2 * slab - 1)) & 7


def sent_range(slab, offset):
    low = 2 * (slab & 1)
    return (offset >= low) & (offset <= low + 2)


def gather_resid(slab, slabs, mine, mate, beside, relayed, height, breadth, visit):
    offset = plane_offset(slab, (8, breadth))
    odd = slab & 1
    edge = slab + 1 - 2 * odd
    from_beside = sent_range(slab, offset) & (slab > 0) & (slab < slabs - 1)
    from_relay = (offset == 4 * (1 - odd)) & (edge > 0) & (edge < slabs - 1)
    plane = 2 * slab - 1 + offset
    valid = (offset < 5) & (plane >= 0) & (plane < 2 * slabs)
    if relayed is None:
        valid &= offset != 4 * (1 - odd)
    for y in range(height):
        cols = slice(y * breadth, (y + 1) * breadth)
        near = beside[:, cols]
        total = mine[:, cols] + mate[:, cols]
        total += jnp.where(from_beside, jnp.concatenate([near, near], axis=0), 0.0)
        if relayed is not None:
            far = relayed[:, cols]
            total += jnp.where(from_relay, jnp.concatenate([far, far], axis=0), 0.0)
        visit(y, jnp.where(valid, total, 0.0))


def unfold(resid, unfolded, height, breadth, y):
    lane = iota((8, breadth), 1)
    shifted = [
        jnp.where(lane >= 1, pltpu.roll(resid, 1, 1), 0.0),
        resid,
        jnp.where(lane < breadth - 1, pltpu.roll(resid, breadth - 1, 1), 0.0),
        jnp.where(lane < breadth - 2, pltpu.roll(resid, breadth - 2, 1), 0.0),
    ]
    halves = [jnp.concatenate(shifted[k : k + 2], axis=0).astype(BF16) for k in (0, 2)]
    for row in range(4):
        target = y - row + 1
        if 0 <= target < height:
            for k in range(2):
                start = row * 32 + k * 16
                unfolded[start : start + 16, target * breadth : (target + 1) * breadth] = halves[k]


def unfold_edges(unfolded, height, breadth):
    zeros = jnp.zeros((32, breadth), BF16)
    for row in range(4):
        for y in range(height):
            if not 0 <= y + row - 1 < height:
                unfolded[row * 32 : row * 32 + 32, y * breadth : (y + 1) * breadth] = zeros


def start_kernel(
    height, breadth, slab_ref, maps, tomo, atoms, limits,
    share, by_voxel, rows_out, cols_out, tomo_out, limits_out,
    natural, bank_in, limits_in, wide, products, sems,
):
    slab = slab_ref[0]
    atom_count = by_voxel.shape[0] // 2
    half = maps.shape[0] // 2
    copies = [
        pltpu.make_async_copy(atoms, bank_in, sems.at[0]),
        pltpu.make_async_copy(maps.at[:half], natural.at[:half], sems.at[1]),
        pltpu.make_async_copy(maps.at[half:], natural.at[half:], sems.at[2]),
        pltpu.make_async_copy(tomo, tomo_out, sems.at[3]),
        pltpu.make_async_copy(limits, limits_in, sems.at[4]),
    ]
    for copy in copies:
        copy.start()
    copies[0].wait()
    bank = bank_in[...].astype(BF16)
    rows_out[...] = bank_rows(bank, slab)
    cols = bank_cols(bank, slab)
    cols_out[...] = cols
    group = atom_count // 2
    for part in range(2):
        copies[1 + part].wait()
        span = slice(part * half, (part + 1) * half)
        wide[span, :] = natural[span, :].astype(F32)
        for y in range(height):
            for z in range(2):
                rows = wide[pl.ds(part * half + z * height + y, group, stride=2 * height), :]
                first = z * atom_count + part * group
                by_voxel[first : first + group, y * breadth : (y + 1) * breadth] = rows.astype(BF16)
    copies[3].wait()
    copies[4].wait()
    square = (atom_count, atom_count)
    column = jnp.sum(jnp.where(iota(square, 0) == iota(square, 1), limits_in[...], 0.0), axis=1, keepdims=True)
    limits_out[...] = jnp.broadcast_to(jnp.concatenate([column, column], axis=0), limits_out.shape)
    spread([(cols, by_voxel)], products, height, breadth, emit_share(slab, tomo_out, share, height, breadth))


def relay_kernel(slab_ref, mine, mate, out):
    slab = slab_ref[0]
    total = mine[...] + mate[...]
    total = jnp.where(sent_range(slab, plane_offset(slab, total.shape)), total, 0.0)
    out[...] = total[:4] + total[4:]


def step_kernel(
    height, breadth, slabs, last, slab_ref, mine, mate, beside, relayed, maps, tomo, rows, cols, limits,
    share, by_voxel, unfolded, products,
):
    slab = slab_ref[0]
    size = height * breadth
    unfold_edges(unfolded, height, breadth)
    gather_resid(
        slab, slabs, mine, mate, beside, relayed, height, breadth,
        lambda y, resid: unfold(resid, unfolded, height, breadth, y),
    )
    limit = jnp.concatenate([limits[...]] * (CHUNK // limits.shape[1]), axis=1)
    bank = rows[...]
    for start in range(0, size, CHUNK):
        part = slice(start, start + CHUNK)
        gradient = jnp.dot(bank, unfolded[:, part], preferred_element_type=F32)
        before = maps[:, part].astype(F32)
        moved = before - coef_step * gradient
        after = (moved - jnp.clip(moved, -limit, limit)).astype(BF16)
        if not last:
            after = after.astype(F32)
            after = (after + momentum * (after - before)).astype(BF16)
        by_voxel[:, part] = after
    spread([(cols[...], by_voxel)], products, height, breadth, emit_share(slab, tomo, share, height, breadth))


def natural_kernel(height, breadth, maps, natural, wide):
    atom_count = maps.shape[0] // 2
    for y in range(height):
        rows = maps[:, y * breadth : (y + 1) * breadth].astype(F32)
        for z in range(2):
            wide[pl.ds(z * height + y, atom_count, stride=2 * height), :] = rows[z * atom_count : (z + 1) * atom_count]
    natural[...] = wide[...].astype(BF16)


def descent_kernel(
    height, breadth, slabs, slab_ref, mine, mate, beside, maps, mate_maps, packed, resid_out, unfolded, planes
):
    slab = slab_ref[0]
    odd = slab & 1
    atom_count = maps.shape[0] // 2
    unfold_edges(unfolded, height, breadth)

    def visit(y, resid):
        planes[8 * y : 8 * y + 8, :] = resid
        unfold(resid, unfolded, height, breadth, y)

    gather_resid(slab, slabs, mine, mate, beside, None, height, breadth, visit)
    for z in range(2):
        resid_out[z * height : (z + 1) * height, :] = planes[pl.ds((2 * slab + z) & 7, height, stride=8), :]
    start = pl.multiple_of(odd * atom_count, atom_count)
    terms = [
        (taps_dot(maps[...], unfolded[...], ((1,), (1,))), 0, False),
        (taps_dot(mate_maps[pl.ds(start, atom_count), :], unfolded[...], ((1,), (1,))), 2 - 3 * odd, True),
    ]
    tap = iota((128, 64), 1) >> 4
    total = jnp.zeros((atom_count, 64), F32)
    for both, plane, edge in terms:
        for z in range(both.shape[0] // atom_count):
            left = both[z * atom_count : (z + 1) * atom_count, :]
            pick = tap_select(slab, plane + z, (128, 64), 1)
            if edge:
                pick = jnp.where(tap == 3 * odd, pick, jnp.zeros_like(pick))
            for _ in range(3):
                head = left.astype(BF16)
                total += taps_dot(head, pick, ((1,), (0,)))
                left = left - head.astype(F32)
    half = atom_count // 2
    packed[...] = jnp.concatenate([total[:half], total[half:]], axis=1)


def sum_refs(refs):
    terms = [ref[...] for ref in refs]
    while len(terms) > 1:
        terms = [sum(terms[k + 1 : k + 2], terms[k]) for k in range(0, len(terms), 2)]
    return terms[0]


def sum_kernel(*refs):
    refs[-1][...] = sum_refs(refs[:-1])


def probe_kernel(height, breadth, slabs, slab_ref, maps, mate_maps, beside_maps, *rest):
    *shares, descent_out, norms, products, folded = rest
    slab = slab_ref[0]
    packed = sum_refs(shares)
    descent = jnp.concatenate([packed[:, :64], packed[:, 64:]], axis=0)
    descent_out[...] = descent
    half = descent.astype(BF16)
    row = iota((8, breadth), 0)
    own = (row == ((2 * slab) & 7)) | (row == ((2 * slab + 1) & 7))
    odd = slab & 1
    folded[...] = jnp.zeros_like(folded)

    def emit(y, total):
        folded[...] += jnp.where(own, total * total, 0.0)

    beside_bank = bank_cols(half, slab - 1 + 2 * odd)
    pairs = [
        (bank_cols(half, slab), maps),
        (bank_cols(half, slab + 1 - 2 * odd), mate_maps),
        (jnp.where((slab > 0) & (slab < slabs - 1), beside_bank, jnp.zeros_like(beside_bank)), beside_maps),
    ]
    spread(pairs, products, height, breadth, emit)
    total = jnp.sum(jnp.sum(folded[...], axis=1, keepdims=True), axis=0, keepdims=True)
    norms[...] = jnp.broadcast_to(total, norms.shape)


def call(kernel, outs, operands, scratch=(), spaces=None):
    spaces = spaces or [pltpu.SMEM] + [pltpu.VMEM] * (len(operands) - 1)
    return pl.pallas_call(
        kernel,
        out_shape=[jax.ShapeDtypeStruct(shape, dtype) for shape, dtype in outs],
        in_specs=[pl.BlockSpec(memory_space=space) for space in spaces],
        out_specs=[pl.BlockSpec(memory_space=pltpu.VMEM)] * len(outs),
        scratch_shapes=[pltpu.VMEM(*item) if isinstance(item, tuple) else item for item in scratch],
        compiler_params=pltpu.CompilerParams(vmem_limit_bytes=VMEM_LIMIT),
    )(*operands)


def per_device(tomogram, initial_maps, dictionary, thresholds):
    slabs = lax.axis_size("gz")
    planes, height, breadth = tomogram.shape
    atom_count = initial_maps.shape[0]
    size = height * breadth
    slab = lax.axis_index("gz").astype(jnp.int32).reshape(1)
    tomo = tomogram.reshape(planes * height, breadth)
    natural = initial_maps.reshape(atom_count * planes * height, breadth)
    limits = thresholds.reshape(1, atom_count)
    natural, tomo, dictionary, limits = (
        pltpu.with_memory_space_constraint(x, pltpu.HBM) for x in (natural, tomo, dictionary, limits)
    )

    mates = [(i, i ^ 1) for i in range(slabs)]
    parts = lax.axis_size("vol")
    besides = [(v * slabs + i, v * slabs + i + 1) for v in range(parts) for i in range(1, slabs - 1, 2)]
    besides += [(v * slabs + i, (v + 1) * slabs + i) for v in range(0, parts - 1, 2) for i in (0, slabs - 1)]
    besides += [(j, i) for i, j in besides]

    def to_mate(x):
        return lax.ppermute(x, "gz", mates)

    def to_beside(x):
        return lax.ppermute(x, ("vol", "gz"), besides)

    share_shape = ((8, size), F32)
    maps_shape = ((2 * atom_count, size), BF16)
    natural_shape = (natural.shape, BF16)
    products = ((128, size + 3 * breadth), F32)
    unfolded = ((128, size), BF16)
    wide = (natural.shape, F32)

    def meet(mine):
        mate = to_mate(mine)
        (send,) = call(relay_kernel, [((4, size), F32)], (slab, mine, mate))
        return mine, mate, send

    def step(share, maps, last):
        mine, mate, send = meet(share)
        beside = to_beside(send)
        return call(
            functools.partial(step_kernel, height, breadth, slabs, last),
            [share_shape, maps_shape],
            (slab, mine, mate, beside, to_mate(beside), maps, tomo, rows, cols, limits),
            [unfolded, products],
        )

    share, maps, rows, cols, tomo, limits = call(
        functools.partial(start_kernel, height, breadth),
        [
            share_shape,
            maps_shape,
            ((2 * atom_count, 128), BF16),
            ((128, 2 * atom_count), BF16),
            (tomo.shape, F32),
            ((2 * atom_count, 128), F32),
        ],
        (slab, natural, tomo, dictionary, limits),
        [
            natural_shape,
            (dictionary.shape, F32),
            (limits.shape, F32),
            wide,
            products,
            pltpu.SemaphoreType.DMA((5,)),
        ],
        [pltpu.SMEM] + [pltpu.HBM] * 4,
    )
    share, maps = step(share, maps, False)
    share, maps = step(share, maps, True)
    mine, mate, send = meet(share)
    send, maps = lax.optimization_barrier((send, maps))
    beside = to_beside(send)
    mate_maps = to_mate(maps)
    beside_maps = to_beside(maps)
    (natural,) = call(
        functools.partial(natural_kernel, height, breadth), [natural_shape], (maps,), [wide], [pltpu.VMEM]
    )
    packed_shape = ((atom_count // 2, 128), F32)
    packed, residual = call(
        functools.partial(descent_kernel, height, breadth, slabs),
        [packed_shape, (tomo.shape, F32)],
        (slab, mine, mate, beside, maps, mate_maps),
        [unfolded, ((8 * height, breadth), F32)],
    )
    shares = [packed]
    stride = 1
    while stride < slabs:
        if len(shares) > 1:
            shares = call(sum_kernel, [packed_shape], shares, (), [pltpu.VMEM] * len(shares))
        shares = [*shares] + [
            lax.ppermute(shares[0], "gz", [(i, i ^ (k * stride)) for i in range(slabs)])
            for k in (3, 2, 1)
            if k * stride < slabs
        ]
        stride *= 4
    descent, norms = call(
        functools.partial(probe_kernel, height, breadth, slabs),
        [((atom_count, 64), F32), ((slabs, 128), F32)],
        (slab, maps, mate_maps, beside_maps, *shares),
        [products, ((8, breadth), F32)],
    )
    norms = lax.all_to_all(norms.reshape(slabs, 1, 128), "gz", 0, 0)
    curvature = jnp.sum(norms[:, :, :1]).reshape(1)
    return (
        natural.reshape(initial_maps.shape),
        descent,
        curvature,
        residual.reshape(tomogram.shape),
    )


def solution(mesh):
    return jax.shard_map(
        per_device,
        mesh=mesh,
        in_specs=(P(("vol", "gz"), None, None), P(None, ("vol", "gz"), None, None), P(), P()),
        out_specs=(
            P(None, ("vol", "gz"), None, None),
            P("vol", None),
            P("vol"),
            P(("vol", "gz"), None, None),
        ),
        check_vma=False,
    )
```

```python
import functools
import math

import jax
import jax.numpy as jnp
from jax import lax
from jax.experimental import pallas as pl
from jax.experimental.pallas import tpu as pltpu
from jax.sharding import PartitionSpec as P

coef_step = 0.015
second_t = (1.0 + math.sqrt(5.0)) / 2.0
third_t = (1.0 + math.sqrt(1.0 + 4.0 * second_t * second_t)) / 2.0
momentum = (second_t - 1.0) / third_t

F32 = jnp.float32
BF16 = jnp.bfloat16
CHUNK = 512
VMEM_LIMIT = 16 << 20


def iota(shape, dim):
    return lax.broadcasted_iota(jnp.int32, shape, dim)


def tap_select(slab, plane, shape, tap_dim):
    tap, col = iota(shape, tap_dim), iota(shape, 1 - tap_dim)
    lands = (2 * slab + plane - 1 + (tap >> 4)) & 7
    return (((tap & 15) == (col >> 3)) & (lands == (col & 7))).astype(BF16)


def taps_dot(lhs, rhs, dims):
    return lax.dot_general(lhs, rhs, (dims, ((), ())), preferred_element_type=F32)


def bank_rows(atoms, slab):
    parts = [taps_dot(atoms, tap_select(slab, z, (64, 128), 0), ((1,), (0,))) for z in range(2)]
    return jnp.concatenate(parts, axis=0).astype(BF16)


def bank_cols(atoms, slab):
    parts = [taps_dot(tap_select(slab, z, (128, 64), 1), atoms, ((1,), (1,))) for z in range(2)]
    return jnp.concatenate(parts, axis=1).astype(BF16)


def spread(pairs, products, height, breadth, emit):
    zeros = jnp.zeros((128, 2 * breadth), F32)
    size = height * breadth
    products[:, : 2 * breadth] = zeros
    products[:, 2 * breadth + size :] = zeros[:, :breadth]
    for start in range(0, size, CHUNK):
        part = slice(start, start + CHUNK)
        terms = [jnp.dot(bank, maps[:, part], preferred_element_type=F32) for bank, maps in pairs]
        products[:, 2 * breadth + start : 2 * breadth + start + CHUNK] = sum(terms[1:], terms[0])
    lane = iota((8, breadth), 1)
    for y in range(height):
        sums = []
        for col in range(4):
            terms = [
                products[
                    (4 * row + col) * 8 : (4 * row + col) * 8 + 8,
                    (y + 3 - row) * breadth : (y + 4 - row) * breadth,
                ]
                for row in range(4)
            ]
            sums.append((terms[0] + terms[1]) + (terms[2] + terms[3]))
        total = sums[1] + jnp.where(lane < breadth - 1, pltpu.roll(sums[0], breadth - 1, 1), 0.0)
        total += jnp.where(lane >= 1, pltpu.roll(sums[2], 1, 1), 0.0)
        total += jnp.where(lane >= 2, pltpu.roll(sums[3], 2, 1), 0.0)
        emit(y, total)


def emit_share(slab, tomo, share, height, breadth):
    row = iota((8, breadth), 0)
    first, second = row == ((2 * slab) & 7), row == ((2 * slab + 1) & 7)

    def emit(y, total):
        own = jnp.where(first, tomo[y : y + 1, :], jnp.where(second, tomo[height + y : height + y + 1, :], 0.0))
        share[:, y * breadth : (y + 1) * breadth] = own - total

    return emit


def plane_offset(slab, shape):
    return (iota(shape, 0) - (2 * slab - 1)) & 7


def sent_range(slab, offset):
    low = 2 * (slab & 1)
    return (offset >= low) & (offset <= low + 2)


def gather_resid(slab, slabs, mine, mate, beside, relayed, height, breadth, visit):
    offset = plane_offset(slab, (8, breadth))
    odd = slab & 1
    edge = slab + 1 - 2 * odd
    from_beside = sent_range(slab, offset) & (slab > 0) & (slab < slabs - 1)
    from_relay = (offset == 4 * (1 - odd)) & (edge > 0) & (edge < slabs - 1)
    plane = 2 * slab - 1 + offset
    valid = (offset < 5) & (plane >= 0) & (plane < 2 * slabs)
    if relayed is None:
        valid &= offset != 4 * (1 - odd)
    for y in range(height):
        cols = slice(y * breadth, (y + 1) * breadth)
        near = beside[:, cols]
        total = mine[:, cols] + mate[:, cols]
        total += jnp.where(from_beside, jnp.concatenate([near, near], axis=0), 0.0)
        if relayed is not None:
            far = relayed[:, cols]
            total += jnp.where(from_relay, jnp.concatenate([far, far], axis=0), 0.0)
        visit(y, jnp.where(valid, total, 0.0))


def unfold(resid, unfolded, height, breadth, y):
    lane = iota((8, breadth), 1)
    shifted = [
        jnp.where(lane >= 1, pltpu.roll(resid, 1, 1), 0.0),
        resid,
        jnp.where(lane < breadth - 1, pltpu.roll(resid, breadth - 1, 1), 0.0),
        jnp.where(lane < breadth - 2, pltpu.roll(resid, breadth - 2, 1), 0.0),
    ]
    halves = [jnp.concatenate(shifted[k : k + 2], axis=0).astype(BF16) for k in (0, 2)]
    for row in range(4):
        target = y - row + 1
        if 0 <= target < height:
            for k in range(2):
                start = row * 32 + k * 16
                unfolded[start : start + 16, target * breadth : (target + 1) * breadth] = halves[k]


def unfold_edges(unfolded, height, breadth):
    zeros = jnp.zeros((32, breadth), BF16)
    for row in range(4):
        for y in range(height):
            if not 0 <= y + row - 1 < height:
                unfolded[row * 32 : row * 32 + 32, y * breadth : (y + 1) * breadth] = zeros


def start_kernel(
    height, breadth, slab_ref, maps, tomo, atoms, limits,
    share, by_voxel, rows_out, cols_out, tomo_out, limits_out,
    natural, bank_in, limits_in, wide, products, sems,
):
    slab = slab_ref[0]
    atom_count = by_voxel.shape[0] // 2
    half = maps.shape[0] // 2
    copies = [
        pltpu.make_async_copy(atoms, bank_in, sems.at[0]),
        pltpu.make_async_copy(maps.at[:half], natural.at[:half], sems.at[1]),
        pltpu.make_async_copy(maps.at[half:], natural.at[half:], sems.at[2]),
        pltpu.make_async_copy(tomo, tomo_out, sems.at[3]),
        pltpu.make_async_copy(limits, limits_in, sems.at[4]),
    ]
    for copy in copies:
        copy.start()
    copies[0].wait()
    bank = bank_in[...].astype(BF16)
    rows_out[...] = bank_rows(bank, slab)
    cols = bank_cols(bank, slab)
    cols_out[...] = cols
    group = atom_count // 2
    for part in range(2):
        copies[1 + part].wait()
        span = slice(part * half, (part + 1) * half)
        wide[span, :] = natural[span, :].astype(F32)
        for y in range(height):
            for z in range(2):
                rows = wide[pl.ds(part * half + z * height + y, group, stride=2 * height), :]
                first = z * atom_count + part * group
                by_voxel[first : first + group, y * breadth : (y + 1) * breadth] = rows.astype(BF16)
    copies[3].wait()
    copies[4].wait()
    square = (atom_count, atom_count)
    column = jnp.sum(jnp.where(iota(square, 0) == iota(square, 1), limits_in[...], 0.0), axis=1, keepdims=True)
    limits_out[...] = jnp.broadcast_to(jnp.concatenate([column, column], axis=0), limits_out.shape)
    spread([(cols, by_voxel)], products, height, breadth, emit_share(slab, tomo_out, share, height, breadth))


def relay_kernel(slab_ref, mine, mate, out):
    slab = slab_ref[0]
    total = mine[...] + mate[...]
    total = jnp.where(sent_range(slab, plane_offset(slab, total.shape)), total, 0.0)
    out[...] = total[:4] + total[4:]


def step_kernel(
    height, breadth, slabs, last, slab_ref, mine, mate, beside, relayed, maps, tomo, rows, cols, limits,
    share, by_voxel, unfolded, products,
):
    slab = slab_ref[0]
    size = height * breadth
    unfold_edges(unfolded, height, breadth)
    gather_resid(
        slab, slabs, mine, mate, beside, relayed, height, breadth,
        lambda y, resid: unfold(resid, unfolded, height, breadth, y),
    )
    limit = jnp.concatenate([limits[...]] * (CHUNK // limits.shape[1]), axis=1)
    bank = rows[...]
    for start in range(0, size, CHUNK):
        part = slice(start, start + CHUNK)
        gradient = jnp.dot(bank, unfolded[:, part], preferred_element_type=F32)
        before = maps[:, part].astype(F32)
        moved = before - coef_step * gradient
        after = (moved - jnp.clip(moved, -limit, limit)).astype(BF16)
        if not last:
            after = after.astype(F32)
            after = (after + momentum * (after - before)).astype(BF16)
        by_voxel[:, part] = after
    spread([(cols[...], by_voxel)], products, height, breadth, emit_share(slab, tomo, share, height, breadth))


def natural_kernel(height, breadth, maps, natural, wide):
    atom_count = maps.shape[0] // 2
    for y in range(height):
        rows = maps[:, y * breadth : (y + 1) * breadth].astype(F32)
        for z in range(2):
            wide[pl.ds(z * height + y, atom_count, stride=2 * height), :] = rows[z * atom_count : (z + 1) * atom_count]
    natural[...] = wide[...].astype(BF16)


def descent_kernel(
    height, breadth, slabs, slab_ref, mine, mate, beside, maps, mate_maps, packed, resid_out, unfolded, planes
):
    slab = slab_ref[0]
    odd = slab & 1
    atom_count = maps.shape[0] // 2
    unfold_edges(unfolded, height, breadth)

    def visit(y, resid):
        planes[8 * y : 8 * y + 8, :] = resid
        unfold(resid, unfolded, height, breadth, y)

    gather_resid(slab, slabs, mine, mate, beside, None, height, breadth, visit)
    for z in range(2):
        resid_out[z * height : (z + 1) * height, :] = planes[pl.ds((2 * slab + z) & 7, height, stride=8), :]
    start = pl.multiple_of(odd * atom_count, atom_count)
    terms = [
        (taps_dot(maps[...], unfolded[...], ((1,), (1,))), 0, False),
        (taps_dot(mate_maps[pl.ds(start, atom_count), :], unfolded[...], ((1,), (1,))), 2 - 3 * odd, True),
    ]
    tap = iota((128, 64), 1) >> 4
    total = jnp.zeros((atom_count, 64), F32)
    for both, plane, edge in terms:
        for z in range(both.shape[0] // atom_count):
            left = both[z * atom_count : (z + 1) * atom_count, :]
            pick = tap_select(slab, plane + z, (128, 64), 1)
            if edge:
                pick = jnp.where(tap == 3 * odd, pick, jnp.zeros_like(pick))
            for _ in range(3):
                head = left.astype(BF16)
                total += taps_dot(head, pick, ((1,), (0,)))
                left = left - head.astype(F32)
    half = atom_count // 2
    packed[...] = jnp.concatenate([total[:half], total[half:]], axis=1)


def sum_refs(refs):
    terms = [ref[...] for ref in refs]
    while len(terms) > 1:
        terms = [sum(terms[k + 1 : k + 2], terms[k]) for k in range(0, len(terms), 2)]
    return terms[0]


def sum_kernel(*refs):
    refs[-1][...] = sum_refs(refs[:-1])


def probe_kernel(height, breadth, slabs, slab_ref, maps, mate_maps, beside_maps, *rest):
    *shares, descent_out, norms, products, folded = rest
    slab = slab_ref[0]
    packed = sum_refs(shares)
    descent = jnp.concatenate([packed[:, :64], packed[:, 64:]], axis=0)
    descent_out[...] = descent
    half = descent.astype(BF16)
    row = iota((8, breadth), 0)
    own = (row == ((2 * slab) & 7)) | (row == ((2 * slab + 1) & 7))
    odd = slab & 1
    folded[...] = jnp.zeros_like(folded)

    def emit(y, total):
        folded[...] += jnp.where(own, total * total, 0.0)

    beside_bank = bank_cols(half, slab - 1 + 2 * odd)
    pairs = [
        (bank_cols(half, slab), maps),
        (bank_cols(half, slab + 1 - 2 * odd), mate_maps),
        (jnp.where((slab > 0) & (slab < slabs - 1), beside_bank, jnp.zeros_like(beside_bank)), beside_maps),
    ]
    spread(pairs, products, height, breadth, emit)
    total = jnp.sum(jnp.sum(folded[...], axis=1, keepdims=True), axis=0, keepdims=True)
    norms[...] = jnp.broadcast_to(total, norms.shape)


def call(kernel, outs, operands, scratch=(), spaces=None):
    spaces = spaces or [pltpu.SMEM] + [pltpu.VMEM] * (len(operands) - 1)
    return pl.pallas_call(
        kernel,
        out_shape=[jax.ShapeDtypeStruct(shape, dtype) for shape, dtype in outs],
        in_specs=[pl.BlockSpec(memory_space=space) for space in spaces],
        out_specs=[pl.BlockSpec(memory_space=pltpu.VMEM)] * len(outs),
        scratch_shapes=[pltpu.VMEM(*item) if isinstance(item, tuple) else item for item in scratch],
        compiler_params=pltpu.CompilerParams(vmem_limit_bytes=VMEM_LIMIT),
    )(*operands)


def per_device(tomogram, initial_maps, dictionary, thresholds):
    slabs = lax.axis_size("gz")
    planes, height, breadth = tomogram.shape
    atom_count = initial_maps.shape[0]
    size = height * breadth
    slab = lax.axis_index("gz").astype(jnp.int32).reshape(1)
    tomo = tomogram.reshape(planes * height, breadth)
    natural = initial_maps.reshape(atom_count * planes * height, breadth)
    limits = thresholds.reshape(1, atom_count)
    natural, tomo, dictionary, limits = (
        pltpu.with_memory_space_constraint(x, pltpu.HBM) for x in (natural, tomo, dictionary, limits)
    )

    mates = [(i, i ^ 1) for i in range(slabs)]
    parts = lax.axis_size("vol")
    besides = [(v * slabs + i, v * slabs + i + 1) for v in range(parts) for i in range(1, slabs - 1, 2)]
    besides += [(v * slabs + i, (v + 1) * slabs + i) for v in range(0, parts - 1, 2) for i in (0, slabs - 1)]
    besides += [(j, i) for i, j in besides]

    def to_mate(x):
        return lax.ppermute(x, "gz", mates)

    def to_beside(x):
        return lax.ppermute(x, ("vol", "gz"), besides)

    def everywhere(x, strides):
        terms = [x]
        for stride in strides:
            if len(terms) > 1:
                terms = call(sum_kernel, [(x.shape, F32)], terms, (), [pltpu.VMEM] * len(terms))
            terms = list(terms)
            for k in (3, 2, 1):
                if k * stride < slabs:
                    swaps = [(i, i ^ (k * stride)) for i in range(slabs)]
                    terms.append(lax.ppermute(terms[0], "gz", swaps))
        return terms

    strides = [4**k for k in range(slabs.bit_length()) if 4**k < slabs]

    share_shape = ((8, size), F32)
    maps_shape = ((2 * atom_count, size), BF16)
    natural_shape = (natural.shape, BF16)
    products = ((128, size + 3 * breadth), F32)
    unfolded = ((128, size), BF16)
    wide = (natural.shape, F32)

    def meet(mine):
        mate = to_mate(mine)
        (send,) = call(relay_kernel, [((4, size), F32)], (slab, mine, mate))
        return mine, mate, send

    def step(share, maps, last):
        mine, mate, send = meet(share)
        beside = to_beside(send)
        return call(
            functools.partial(step_kernel, height, breadth, slabs, last),
            [share_shape, maps_shape],
            (slab, mine, mate, beside, to_mate(beside), maps, tomo, rows, cols, limits),
            [unfolded, products],
        )

    share, maps, rows, cols, tomo, limits = call(
        functools.partial(start_kernel, height, breadth),
        [
            share_shape,
            maps_shape,
            ((2 * atom_count, 128), BF16),
            ((128, 2 * atom_count), BF16),
            (tomo.shape, F32),
            ((2 * atom_count, 128), F32),
        ],
        (slab, natural, tomo, dictionary, limits),
        [
            natural_shape,
            (dictionary.shape, F32),
            (limits.shape, F32),
            wide,
            products,
            pltpu.SemaphoreType.DMA((5,)),
        ],
        [pltpu.SMEM] + [pltpu.HBM] * 4,
    )
    share, maps = step(share, maps, False)
    share, maps = step(share, maps, True)
    mine, mate, send = meet(share)
    send, maps = lax.optimization_barrier((send, maps))
    beside = to_beside(send)
    mate_maps = to_mate(maps)
    beside_maps = to_beside(maps)
    (natural,) = call(
        functools.partial(natural_kernel, height, breadth), [natural_shape], (maps,), [wide], [pltpu.VMEM]
    )
    packed_shape = ((atom_count // 2, 128), F32)
    packed, residual = call(
        functools.partial(descent_kernel, height, breadth, slabs),
        [packed_shape, (tomo.shape, F32)],
        (slab, mine, mate, beside, maps, mate_maps),
        [unfolded, ((8 * height, breadth), F32)],
    )
    shares = everywhere(packed, strides[::-1])
    descent, norms = call(
        functools.partial(probe_kernel, height, breadth, slabs),
        [((atom_count, 64), F32), ((8, 128), F32)],
        (slab, maps, mate_maps, beside_maps, *shares),
        [products, ((8, breadth), F32)],
    )
    norms = everywhere(norms, strides)
    curvature = sum(norms[1:], norms[0])[0, :1]
    return (
        natural.reshape(initial_maps.shape),
        descent,
        curvature,
        residual.reshape(tomogram.shape),
    )


def solution(mesh):
    return jax.shard_map(
        per_device,
        mesh=mesh,
        in_specs=(P(("vol", "gz"), None, None), P(None, ("vol", "gz"), None, None), P(), P()),
        out_specs=(
            P(None, ("vol", "gz"), None, None),
            P("vol", None),
            P("vol"),
            P(("vol", "gz"), None, None),
        ),
        check_vma=False,
    )
```
